256 devices in a mesh: tile: 16 (over z_hi, y), group: 16 (over x, z_lo, core).
Axes of the slice: x: 4, y: 4, z: 8 (z_hi: 4, z_lo: 2; z = z_hi * 2 + z_lo), core: 2. Of those that a mesh axis runs over, the one named last changes fastest.
Arguments:
- tracers: float32 [128, 16, 128, 256], P('group', None, 'tile'), may hold values from -6 to 6
- emissions: float32 [128, 128, 256], P('group', 'tile'), may hold values from -6 to 6
- winds: float32 [16, 2, 16, 128, 256], P('group', None, None, 'tile'), may hold values from -1.44 to 1.44, as said below
- diffusivity: float32 [16, 15, 128, 256], P('group', None, 'tile'), may hold values from 0.05 to 2
- substeps: int32 [16], replicated, may hold values from 1 to 6, as said below
- loader: int32 [16], replicated, may hold values from 0 to 15
Outputs:
- mixed: float32 [128, 16, 128, 256], P('group', None, 'tile')
The draws below stay inside these ranges and needn't reach their ends.
Inputs may be any that keep to these rules, and one draw needn't show every extreme that they name: The first and the last tile take 6 substeps. `winds`: divided by the substep count of the tile that holds the face (for a meridional value on a tile's first row, by the smaller count of that tile and the tile south of it), every entry lies within -0.24 to 0.24.
All inputs are finite; a program needn't handle non-finite values.
Results may differ from the reference program's by a relative error of at most 0.00002.
Values sent between devices are 32-bit elements; how exact they have to be, the bound alone decides.
A program may use at most 64 MiB of HBM per device.

```python
import math
import jax
import jax.numpy as jnp
from jax import lax

TR_DEV = 8
LEV = 16
LAT_DEV = 8
LON = 256
ROUNDS = 6
TRACERS = 128
LAT = 128
TILES = 16
SLOTS = 16
N_GROUP = 16


def tile_counts(key):
    counts = jax.random.randint(jax.random.fold_in(key, 7), (TILES,), 1, ROUNDS + 1)
    position = jnp.arange(TILES)
    polar = (position == 0) | (position == TILES - 1)
    return jnp.where(polar, ROUNDS, counts).astype(jnp.int32)


def draw_substeps(key, part):
    return tile_counts(key)


def draw_winds(key, part):
    counts = tile_counts(key)
    row_index = jnp.arange(LAT)
    row_tiles = row_index // LAT_DEV
    own_count = counts[row_tiles]
    below_count = counts[jnp.maximum(row_tiles - 1, 0)]
    first_row = row_index % LAT_DEV == 0
    merid_count = jnp.where(first_row, jnp.minimum(own_count, below_count), own_count)
    row_scale = jnp.stack([own_count, merid_count]).astype(jnp.float32)
    draw_shape = (SLOTS, 2, LEV, LAT, LON)
    base_draw = jax.random.uniform(jax.random.fold_in(key, 19), draw_shape, jnp.float32, -0.24, 0.24)
    return (base_draw * row_scale[None, :, None, :, None]).astype(jnp.float32)


def plant(array, own_key, least, largest):
    extent = array.shape
    index_at = [jax.random.randint(jax.random.fold_in(own_key, axis), (), 0, extent[axis]) for axis in range(len(extent))]
    array = array.at[tuple(index_at)].set(least)
    longest = extent.index(max(extent))
    index_at[longest] = (index_at[longest] + 1) % extent[longest]
    return array.at[tuple(index_at)].set(largest)


def shard_levels(key, shape, pieces, least, largest):
    level = 1.0
    for axis_at, shards_of in pieces:
        steps = jax.random.uniform(jax.random.fold_in(jax.random.fold_in(key, 6), axis_at), (shards_of,), jnp.float32, least / len(pieces), largest / len(pieces))
        level = level * jnp.repeat(jnp.exp(steps), shape[axis_at] // shards_of).reshape((-1,) + (1,) * (len(shape) - 1 - axis_at))
    return level


def noise(rng, shape, spread, most, split=(), held_as=jnp.bfloat16):
    gain = shard_levels(rng, shape, split, -0.22, 0.18) if split else 1.0
    array = jax.random.normal(rng, shape, jnp.float32) * spread * gain
    return jnp.minimum(jnp.maximum(array, -most), most).astype(held_as)


def setup_inputs(seed: int = 0) -> dict:
    key_list = jax.random.split(jax.random.key(seed), 7)
    tracers = noise(key_list[0], (TRACERS, LEV, LAT, LON), 1.0, 6.0, ((0, 16), (2, 16)), jnp.float32)
    emissions = noise(key_list[1], (TRACERS, LAT, LON), 1.0, 6.0, ((0, 16), (1, 16)), jnp.float32)
    winds = draw_winds(jax.random.fold_in(key_list[6], 71), 0)
    diffusivity = jnp.clip(jnp.exp(math.log(2.0) - 3.6888794 * jax.random.uniform(key_list[3], (SLOTS, LEV - 1, LAT, LON), jnp.float32) ** shard_levels(key_list[3], (SLOTS, LEV - 1, LAT, LON), ((0, 16), (2, 16)), -0.2, 0.2)), 0.05, 2.0)
    substeps = draw_substeps(jax.random.fold_in(key_list[6], 71), 0)
    loader = plant(jax.random.randint(key_list[5], (TILES,), 0, N_GROUP), jax.random.fold_in(key_list[5], 1), 0, N_GROUP - 1).astype(jnp.int32)
    return dict(tracers=tracers, emissions=emissions, winds=winds, diffusivity=diffusivity, substeps=substeps, loader=loader)


def thomas_solve(mixing, coefficient):
    levels = mixing.shape[1]
    zero_plane = jnp.zeros_like(coefficient[0])
    previous_ratio = zero_plane
    previous_value = jnp.zeros_like(mixing[:, 0])
    ratios = []
    values = []
    for level in range(levels):
        lower_coef = coefficient[level - 1] if level > 0 else zero_plane
        upper_coef = coefficient[level] if level < levels - 1 else zero_plane
        pivot = 1.0 / (1.0 + lower_coef + upper_coef - lower_coef * previous_ratio)
        previous_ratio = upper_coef * pivot
        previous_value = (mixing[:, level] + lower_coef * previous_value) * pivot
        ratios.append(previous_ratio)
        values.append(previous_value)
    solved = [None] * levels
    current = values[levels - 1]
    solved[levels - 1] = current
    for level in range(levels - 2, -1, -1):
        current = values[level] + ratios[level] * current
        solved[level] = current
    return jnp.stack(solved, axis=1)


def advance(mixing, zonal, meridional, fraction):
    from_west = jnp.roll(mixing, 1, axis=3)
    west_flux = jnp.maximum(zonal, 0.0) * from_west + jnp.minimum(zonal, 0.0) * mixing
    east_flux = jnp.roll(west_flux, -1, axis=3)
    zeros_row = jnp.zeros_like(mixing[:, :, :1])
    from_south = jnp.concatenate([zeros_row, mixing[:, :, :-1]], axis=2)
    south_flux = jnp.maximum(meridional, 0.0) * from_south + jnp.minimum(meridional, 0.0) * mixing
    north_flux = jnp.concatenate([south_flux[:, :, 1:], zeros_row], axis=2)
    return mixing - fraction[:, None] * ((east_flux - west_flux) + (north_flux - south_flux))


def reference(tracers, emissions, winds, diffusivity, substeps, loader):
    row_slots = jnp.repeat(loader.astype(jnp.int32), LAT_DEV)
    chosen = jnp.arange(SLOTS, dtype=jnp.int32)[:, None] == row_slots[None, :]
    courant = jnp.sum(jnp.where(chosen[:, None, None, :, None], winds, jnp.zeros_like(winds)), axis=0)
    coefficient = jnp.sum(jnp.where(chosen[:, None, :, None], diffusivity, jnp.zeros_like(diffusivity)), axis=0)
    row_index = jnp.arange(LAT)
    zonal = courant[0]
    meridional = courant[1] * (row_index > 0).astype(courant.dtype)[:, None]
    counts = jnp.repeat(substeps, LAT_DEV)
    counts_float = counts.astype(tracers.dtype)
    blocks = tracers.reshape(N_GROUP, TR_DEV, LEV, LAT, LON)
    sources = emissions.reshape(N_GROUP, TR_DEV, LAT, LON)

    def window(pair):
        mixing, source = pair
        for substep in range(ROUNDS):
            fraction = jnp.where(substep < counts, 1.0 / counts_float, jnp.zeros_like(counts_float))
            mixing = advance(mixing, zonal, meridional, fraction)
        mixing = mixing.at[:, 0].add(source)
        return thomas_solve(mixing, coefficient)

    result = lax.map(window, (blocks, sources))
    return result.reshape(TRACERS, LEV, LAT, LON)
```

```python
import jax
import jax.numpy as jnp
from jax import lax
from jax.sharding import PartitionSpec as P

ROUNDS = 6


def from_behind(value, axis, by):
    count = lax.axis_size(axis)
    pairs = [(i, i + by) for i in range(count) if 0 <= i + by < count]
    return lax.ppermute(value, axis, pairs)


def broadcast_from(value, axis, root):
    count = lax.axis_size(axis)
    assert count & (count - 1) == 0
    distance = lax.axis_index(axis) ^ root
    current = value
    bit = 0
    while (1 << bit) < count:
        pairs = [(i, i ^ (1 << bit)) for i in range(count)]
        received = lax.ppermute(current, axis, pairs)
        current = jnp.where((distance >> bit) == 1, received, current)
        bit += 1
    return current


def thomas_solve(mixing, coefficient):
    levels = mixing.shape[1]
    zero_plane = jnp.zeros_like(coefficient[0])
    previous_ratio = zero_plane
    previous_value = jnp.zeros_like(mixing[:, 0])
    ratios = []
    values = []
    for level in range(levels):
        lower_coef = coefficient[level - 1] if level > 0 else zero_plane
        upper_coef = coefficient[level] if level < levels - 1 else zero_plane
        pivot = 1.0 / (1.0 + lower_coef + upper_coef - lower_coef * previous_ratio)
        previous_ratio = upper_coef * pivot
        previous_value = (mixing[:, level] + lower_coef * previous_value) * pivot
        ratios.append(previous_ratio)
        values.append(previous_value)
    solved = [None] * levels
    current = values[levels - 1]
    solved[levels - 1] = current
    for level in range(levels - 2, -1, -1):
        current = values[level] + ratios[level] * current
        solved[level] = current
    return jnp.stack(solved, axis=1)


def advance(mixing, zonal, meridional, fraction):
    from_west = jnp.roll(mixing, 1, axis=3)
    west_flux = jnp.maximum(zonal, 0.0) * from_west + jnp.minimum(zonal, 0.0) * mixing
    east_flux = jnp.roll(west_flux, -1, axis=3)
    zeros_row = jnp.zeros_like(mixing[:, :, :1])
    from_south = jnp.concatenate([zeros_row, mixing[:, :, :-1]], axis=2)
    south_flux = jnp.maximum(meridional, 0.0) * from_south + jnp.minimum(meridional, 0.0) * mixing
    north_flux = jnp.concatenate([south_flux[:, :, 1:], zeros_row], axis=2)
    return mixing - fraction * ((east_flux - west_flux) + (north_flux - south_flux))


def shards(tracers, emissions, winds, diffusivity, substeps, loader):
    tiles = lax.axis_size("tile")
    tile_position = lax.axis_index("tile")
    tile_numbers = jnp.arange(substeps.shape[0])
    loader_slot = jnp.sum(jnp.where(tile_numbers == tile_position, loader, 0))
    levels = tracers.shape[1]
    height = tracers.shape[2]
    width = tracers.shape[3]
    halo = ROUNDS

    local = jnp.concatenate(
        [winds[0].reshape(2 * levels, height, width), diffusivity[0]], axis=0
    )
    chosen = broadcast_from(local, "group", loader_slot)
    courant = chosen[: 2 * levels]
    coefficient = chosen[2 * levels :]

    south_tracers = from_behind(tracers[:, :, height - halo :], "tile", 1)
    north_tracers = from_behind(tracers[:, :, :halo], "tile", -1)
    south_courant = from_behind(courant[:, height - halo :], "tile", 1)
    north_courant = from_behind(courant[:, :halo], "tile", -1)

    row_global = tile_position * height + jnp.arange(height)
    own_mask = (row_global > 0).astype(jnp.float32)[:, None]
    zonal = jnp.concatenate(
        [south_courant[:levels], courant[:levels], north_courant[:levels]], axis=1
    )
    meridional = jnp.concatenate(
        [
            south_courant[levels:],
            courant[levels:] * own_mask,
            north_courant[levels:],
        ],
        axis=1,
    )
    mixing = jnp.concatenate([south_tracers, tracers, north_tracers], axis=2)

    def count_of(position):
        clamped = jnp.clip(position, 0, tiles - 1)
        return jnp.sum(jnp.where(tile_numbers == clamped, substeps, 0))

    row_counts = jnp.concatenate(
        [
            jnp.full((halo,), count_of(tile_position - 1)),
            jnp.full((height,), count_of(tile_position)),
            jnp.full((halo,), count_of(tile_position + 1)),
        ]
    )
    counts_float = row_counts.astype(jnp.float32)
    for substep in range(ROUNDS):
        fraction = jnp.where(substep < row_counts, 1.0 / counts_float, jnp.float32(0.0))
        mixing = advance(mixing, zonal, meridional, fraction[:, None])
    mixing = mixing[:, :, halo : halo + height]
    mixing = mixing.at[:, 0].add(emissions)
    return thomas_solve(mixing, coefficient)


def solution(mesh):
    return jax.shard_map(
        shards,
        mesh=mesh,
        in_specs=(
            P("group", None, "tile", None),
            P("group", "tile", None),
            P("group", None, None, "tile", None),
            P("group", None, "tile", None),
            P(),
            P(),
        ),
        out_specs=P("group", None, "tile", None),
        check_vma=False,
    )
```

```python
import jax
import jax.numpy as jnp
from jax import lax
from jax.experimental import pallas as pl
from jax.experimental.pallas import tpu as pltpu
from jax.sharding import PartitionSpec as P

ROUNDS = 6


def from_behind(value, axis, by):
    count = lax.axis_size(axis)
    pairs = [(i, i + by) for i in range(count) if 0 <= i + by < count]
    return lax.ppermute(value, axis, pairs)


def broadcast_from(value, axis, root):
    count = lax.axis_size(axis)
    assert count & (count - 1) == 0
    distance = lax.axis_index(axis) ^ root
    current = value
    bit = 0
    while (1 << bit) < count:
        pairs = [(i, i ^ (1 << bit)) for i in range(count)]
        received = lax.ppermute(current, axis, pairs)
        current = jnp.where((distance >> bit) == 1, received, current)
        bit += 1
    return current


def transport_kernel(
    scalars, own, north, south, courant, north_courant, south_courant, coefficient,
    emissions, out, zonal_up, zonal_down, merid_up, merid_down, fractions, pivots,
    ratios, held,
):
    levels = own.shape[1]
    height = own.shape[2]
    width = own.shape[3]
    extent = 3 * height

    @pl.when(pl.program_id(0) == 0)
    def _prepare():
        row = lax.broadcasted_iota(jnp.int32, (extent, width), 0)
        for substep in range(ROUNDS):
            fractions[substep] = jnp.where(
                row < height,
                scalars[3 * substep],
                jnp.where(row < 2 * height, scalars[3 * substep + 1], scalars[3 * substep + 2]),
            )
        own_row = lax.broadcasted_iota(jnp.int32, (height, width), 0)
        mask = jnp.where(own_row == 0, scalars[3 * ROUNDS], jnp.float32(1.0))
        for level in range(levels):
            zonal = jnp.concatenate(
                [courant[level], north_courant[level], south_courant[level]], axis=0
            )
            meridional = jnp.concatenate(
                [
                    courant[levels + level] * mask,
                    north_courant[levels + level],
                    south_courant[levels + level],
                ],
                axis=0,
            )
            zonal_up[level] = jnp.maximum(zonal, 0.0)
            zonal_down[level] = jnp.minimum(zonal, 0.0)
            merid_up[level] = jnp.maximum(meridional, 0.0)
            merid_down[level] = jnp.minimum(meridional, 0.0)
        zero_plane = jnp.zeros((height, width), jnp.float32)
        previous_ratio = zero_plane
        for level in range(levels):
            lower_coef = coefficient[level - 1] if level > 0 else zero_plane
            upper_coef = coefficient[level] if level < levels - 1 else zero_plane
            pivot = 1.0 / (1.0 + lower_coef + upper_coef - lower_coef * previous_ratio)
            previous_ratio = upper_coef * pivot
            pivots[level] = pivot
            ratios[level] = previous_ratio

    def advect(level, carry):
        mixing = jnp.concatenate([own[0, level], north[0, level], south[0, level]], axis=0)
        z_up = zonal_up[level]
        z_down = zonal_down[level]
        m_up = merid_up[level]
        m_down = merid_down[level]
        for substep in range(ROUNDS):
            from_west = pltpu.roll(mixing, 1, 1)
            west_flux = z_up * from_west + z_down * mixing
            east_flux = pltpu.roll(west_flux, width - 1, 1)
            from_south = pltpu.roll(mixing, 1, 0)
            south_flux = m_up * from_south + m_down * mixing
            north_flux = pltpu.roll(south_flux, extent - 1, 0)
            mixing = mixing - fractions[substep] * (
                (east_flux - west_flux) + (north_flux - south_flux)
            )
        held[level] = mixing[:height]
        return carry

    lax.fori_loop(0, levels, advect, 0)
    held[0] = held[0] + emissions[0]
    zero_plane = jnp.zeros((height, width), jnp.float32)
    previous_value = zero_plane
    for level in range(levels):
        lower_coef = coefficient[level - 1] if level > 0 else zero_plane
        previous_value = (held[level] + lower_coef * previous_value) * pivots[level]
        held[level] = previous_value
    current = held[levels - 1]
    out[0, levels - 1] = current
    for level in range(levels - 2, -1, -1):
        current = held[level] + ratios[level] * current
        out[0, level] = current


def transport(scalars, tracers, north, south, courant, north_courant, south_courant,
              coefficient, emissions):
    tracer_count, levels, height, width = tracers.shape
    extent = 3 * height
    block = pl.BlockSpec((1, levels, height, width), lambda i: (i, 0, 0, 0))

    def whole(shape):
        return pl.BlockSpec(shape, lambda i: (0,) * len(shape))

    plane = pltpu.VMEM((levels, extent, width), jnp.float32)
    return pl.pallas_call(
        transport_kernel,
        grid=(tracer_count,),
        out_shape=jax.ShapeDtypeStruct(tracers.shape, jnp.float32),
        in_specs=[
            pl.BlockSpec(memory_space=pltpu.SMEM),
            block,
            block,
            block,
            whole(courant.shape),
            whole(courant.shape),
            whole(courant.shape),
            whole(coefficient.shape),
            pl.BlockSpec((1, height, width), lambda i: (i, 0, 0)),
        ],
        out_specs=block,
        scratch_shapes=[
            plane,
            plane,
            plane,
            plane,
            pltpu.VMEM((ROUNDS, extent, width), jnp.float32),
            pltpu.VMEM((levels, height, width), jnp.float32),
            pltpu.VMEM((levels, height, width), jnp.float32),
            pltpu.VMEM((levels, height, width), jnp.float32),
        ],
        cost_estimate=pl.CostEstimate(
            flops=tracer_count * levels * extent * width * ROUNDS * 14,
            bytes_accessed=4 * (5 * tracers.size + 3 * courant.size),
            transcendentals=0,
        ),
    )(scalars, tracers, north, south, courant, north_courant, south_courant,
      coefficient, emissions)


def shards(tracers, emissions, winds, diffusivity, substeps, loader):
    tiles = lax.axis_size("tile")
    tile_position = lax.axis_index("tile")
    tile_numbers = jnp.arange(substeps.shape[0])
    loader_slot = jnp.sum(jnp.where(tile_numbers == tile_position, loader, 0))
    levels = tracers.shape[1]
    height = tracers.shape[2]
    width = tracers.shape[3]

    local = jnp.concatenate(
        [winds[0].reshape(2 * levels, height, width), diffusivity[0]], axis=0
    )
    chosen = broadcast_from(local, "group", loader_slot)
    courant = chosen[: 2 * levels]
    coefficient = chosen[2 * levels :]

    south_tracers = from_behind(tracers, "tile", 1)
    north_tracers = from_behind(tracers, "tile", -1)
    south_courant = from_behind(courant, "tile", 1)
    north_courant = from_behind(courant, "tile", -1)

    def count_of(position):
        clamped = jnp.clip(position, 0, tiles - 1)
        return jnp.sum(jnp.where(tile_numbers == clamped, substeps, 0))

    counts = jnp.stack(
        [count_of(tile_position), count_of(tile_position + 1), count_of(tile_position - 1)]
    )
    counts_float = counts.astype(jnp.float32)
    steps = jnp.arange(ROUNDS)[:, None]
    fractions = jnp.where(steps < counts[None, :], 1.0 / counts_float[None, :], jnp.float32(0.0))
    first_row = jnp.where(tile_position > 0, jnp.float32(1.0), jnp.float32(0.0))
    scalars = jnp.concatenate([fractions.reshape(-1), first_row[None]])
    return transport(
        scalars, tracers, north_tracers, south_tracers, courant, north_courant,
        south_courant, coefficient, emissions,
    )


def solution(mesh):
    return jax.shard_map(
        shards,
        mesh=mesh,
        in_specs=(
            P("group", None, "tile", None),
            P("group", "tile", None),
            P("group", None, None, "tile", None),
            P("group", None, "tile", None),
            P(),
            P(),
        ),
        out_specs=P("group", None, "tile", None),
        check_vma=False,
    )
```

```python
import jax
import jax.numpy as jnp
from jax import lax
from jax.experimental import pallas as pl
from jax.experimental.pallas import tpu as pltpu
from jax.sharding import PartitionSpec as P

ROUNDS = 6


def from_behind(value, axis, by):
    count = lax.axis_size(axis)
    pairs = [(i, i + by) for i in range(count) if 0 <= i + by < count]
    return lax.ppermute(value, axis, pairs)


def broadcast_from(value, axis, root):
    count = lax.axis_size(axis)
    assert count & (count - 1) == 0
    distance = lax.axis_index(axis) ^ root
    current = value
    bit = 0
    while (1 << bit) < count:
        pairs = [(i, i ^ (1 << bit)) for i in range(count)]
        received = lax.ppermute(current, axis, pairs)
        current = jnp.where((distance >> bit) == 1, received, current)
        bit += 1
    return current


def transport_kernel(
    scalars, own, south, north, courant, south_courant, north_courant, coefficient,
    emissions, out, held, pivots, ratios, lowers, planes,
):
    height, _, tracer_count, width = own.shape
    levels = held.shape[0]
    halo = south.shape[0]
    rows = height + 2 * halo
    level = pl.program_id(0)
    lane_shape = (tracer_count, width)

    def spread(row_ref, row):
        return jnp.broadcast_to(row_ref[pl.ds(row, 1), :], lane_shape)

    @pl.when(level == 0)
    def _prepare():
        zero_plane = jnp.zeros((height, width), jnp.float32)
        previous_ratio = zero_plane
        for lev in range(levels):
            lower_coef = coefficient[lev - 1] if lev > 0 else zero_plane
            upper_coef = coefficient[lev] if lev < levels - 1 else zero_plane
            pivot = 1.0 / (1.0 + lower_coef + upper_coef - lower_coef * previous_ratio)
            previous_ratio = upper_coef * pivot
            planes[0] = pivot
            planes[1] = previous_ratio
            planes[2] = lower_coef
            for row in range(height):
                pivots[lev, row] = spread(planes.at[0], row)
                ratios[lev, row] = spread(planes.at[1], row)
                lowers[lev, row] = spread(planes.at[2], row)

    def wind_row(component, row):
        index = component * levels + level
        if row < halo:
            return spread(south_courant.at[index], row)
        if row < halo + height:
            return spread(courant.at[index], row - halo)
        return spread(north_courant.at[index], row - halo - height)

    first_row = scalars[3 * ROUNDS]
    zonal_up, zonal_down, merid_up, merid_down = [], [], [], []
    for row in range(rows):
        zonal = wind_row(0, row)
        meridional = wind_row(1, row)
        if row == halo:
            meridional = meridional * first_row
        zonal_up.append(jnp.maximum(zonal, 0.0))
        zonal_down.append(jnp.minimum(zonal, 0.0))
        merid_up.append(jnp.maximum(meridional, 0.0))
        merid_down.append(jnp.minimum(meridional, 0.0))

    mixing = [south[row, 0] for row in range(halo)]
    mixing += [own[row, 0] for row in range(height)]
    mixing += [north[row, 0] for row in range(halo)]
    for substep in range(ROUNDS):
        low, high = substep + 1, rows - 2 - substep
        south_flux = {}
        for row in range(low, high + 2):
            south_flux[row] = merid_up[row] * mixing[row - 1] + merid_down[row] * mixing[row]
        advanced = list(mixing)
        for row in range(low, high + 1):
            band = 0 if row < halo else (1 if row < halo + height else 2)
            fraction = scalars[3 * substep + band]
            from_west = pltpu.roll(mixing[row], 1, 1)
            west_flux = zonal_up[row] * from_west + zonal_down[row] * mixing[row]
            east_flux = pltpu.roll(west_flux, width - 1, 1)
            advanced[row] = mixing[row] - fraction * (
                (east_flux - west_flux) + (south_flux[row + 1] - south_flux[row])
            )
        mixing = advanced
    for row in range(height):
        held[level, row] = mixing[halo + row]

    @pl.when(level == levels - 1)
    def _finish():
        for row in range(height):
            held[0, row] = held[0, row] + emissions[row]
            previous_value = jnp.zeros(lane_shape, jnp.float32)
            for lev in range(levels):
                previous_value = (
                    held[lev, row] + lowers[lev, row] * previous_value
                ) * pivots[lev, row]
                held[lev, row] = previous_value
            current = held[levels - 1, row]
            out[row, levels - 1] = current
            for lev in range(levels - 2, -1, -1):
                current = held[lev, row] + ratios[lev, row] * current
                out[row, lev] = current


def transport(scalars, own, south, north, courant, south_courant, north_courant,
              coefficient, emissions):
    height, levels, tracer_count, width = own.shape
    halo = south.shape[0]

    def whole(shape):
        return pl.BlockSpec(shape, lambda i: (0,) * len(shape))

    def by_level(shape):
        return pl.BlockSpec((shape[0], 1) + shape[2:], lambda i: (0, i, 0, 0))

    table = pltpu.VMEM((levels, height, tracer_count, width), jnp.float32)
    return pl.pallas_call(
        transport_kernel,
        grid=(levels,),
        out_shape=jax.ShapeDtypeStruct(own.shape, jnp.float32),
        in_specs=[
            pl.BlockSpec(memory_space=pltpu.SMEM),
            by_level(own.shape),
            by_level(south.shape),
            by_level(north.shape),
            whole(courant.shape),
            whole(south_courant.shape),
            whole(north_courant.shape),
            whole(coefficient.shape),
            whole(emissions.shape),
        ],
        out_specs=whole(own.shape),
        scratch_shapes=[
            table,
            table,
            table,
            table,
            pltpu.VMEM((3, height, width), jnp.float32),
        ],
        cost_estimate=pl.CostEstimate(
            flops=levels * tracer_count * width * 78 * 14,
            bytes_accessed=4 * (3 * own.size + 2 * south.size + 3 * courant.size),
            transcendentals=0,
        ),
    )(scalars, own, south, north, courant, south_courant, north_courant,
      coefficient, emissions)


def shards(tracers, emissions, winds, diffusivity, substeps, loader):
    tiles = lax.axis_size("tile")
    tile_position = lax.axis_index("tile")
    tile_numbers = jnp.arange(substeps.shape[0])
    loader_slot = jnp.sum(jnp.where(tile_numbers == tile_position, loader, 0))
    levels = tracers.shape[1]
    height = tracers.shape[2]
    width = tracers.shape[3]
    halo = ROUNDS

    local = jnp.concatenate(
        [winds[0].reshape(2 * levels, height, width), diffusivity[0]], axis=0
    )
    chosen = broadcast_from(local, "group", loader_slot)
    courant = chosen[: 2 * levels]
    coefficient = chosen[2 * levels :]

    by_row = jnp.transpose(tracers, (2, 1, 0, 3))
    south_rows = from_behind(by_row[height - halo :], "tile", 1)
    north_rows = from_behind(by_row[:halo], "tile", -1)
    south_courant = from_behind(courant[:, height - halo :], "tile", 1)
    north_courant = from_behind(courant[:, :halo], "tile", -1)

    def count_of(position):
        clamped = jnp.clip(position, 0, tiles - 1)
        return jnp.sum(jnp.where(tile_numbers == clamped, substeps, 0))

    counts = jnp.stack(
        [count_of(tile_position - 1), count_of(tile_position), count_of(tile_position + 1)]
    )
    counts_float = counts.astype(jnp.float32)
    steps = jnp.arange(ROUNDS)[:, None]
    fractions = jnp.where(steps < counts[None, :], 1.0 / counts_float[None, :], jnp.float32(0.0))
    first_row = jnp.where(tile_position > 0, jnp.float32(1.0), jnp.float32(0.0))
    scalars = jnp.concatenate([fractions.reshape(-1), first_row[None]])
    mixed = transport(
        scalars, by_row, south_rows, north_rows, courant, south_courant,
        north_courant, coefficient, jnp.transpose(emissions, (1, 0, 2)),
    )
    return jnp.transpose(mixed, (2, 1, 0, 3))


def solution(mesh):
    return jax.shard_map(
        shards,
        mesh=mesh,
        in_specs=(
            P("group", None, "tile", None),
            P("group", "tile", None),
            P("group", None, None, "tile", None),
            P("group", None, "tile", None),
            P(),
            P(),
        ),
        out_specs=P("group", None, "tile", None),
        check_vma=False,
    )
```

```python
import jax
import jax.numpy as jnp
from jax import lax
from jax.experimental import pallas as pl
from jax.experimental.pallas import tpu as pltpu
from jax.sharding import PartitionSpec as P

ROUNDS = 6


def from_behind(value, axis, by):
    count = lax.axis_size(axis)
    pairs = [(i, i + by) for i in range(count) if 0 <= i + by < count]
    return lax.ppermute(value, axis, pairs)


def spread_kernel(data, out, *scratch):
    bits = len(scratch) - 3
    received = scratch[:bits]
    send_sems, recv_sems, credits = scratch[bits:]
    me = lax.axis_index("group")
    tile = lax.axis_index("tile")

    def partner(bit):
        return me + (1 << bit) * (1 - 2 * ((me // (1 << bit)) % 2))

    barrier = pltpu.get_barrier_semaphore()
    for bit in range(bits):
        pl.semaphore_signal(
            barrier, 1, device_id=(tile, partner(bit)), device_id_type=pl.DeviceIdType.MESH
        )
    pl.semaphore_wait(barrier, bits)
    out[...] = data[...]
    start = 0
    size = out.shape[0]
    for bit in range(bits):
        half = size // 2
        side = (me // (1 << bit)) % 2
        keep = start + side * half
        give = start + (1 - side) * half
        copy = pltpu.make_async_remote_copy(
            src_ref=out.at[pl.ds(give, half)],
            dst_ref=received[bit],
            send_sem=send_sems.at[bit],
            recv_sem=recv_sems.at[bit],
            device_id=(tile, partner(bit)),
            device_id_type=pl.DeviceIdType.MESH,
        )
        copy.start()
        copy.wait()
        pl.semaphore_signal(
            credits.at[bit], 1, device_id=(tile, partner(bit)),
            device_id_type=pl.DeviceIdType.MESH,
        )
        out[pl.ds(keep, half)] = out[pl.ds(keep, half)] + received[bit][...]
        start = keep
        size = half
    for step, bit in enumerate(reversed(range(bits))):
        side = (me // (1 << bit)) % 2
        pl.semaphore_wait(credits.at[bit], 1)
        copy = pltpu.make_async_remote_copy(
            src_ref=out.at[pl.ds(start, size)],
            dst_ref=out.at[pl.ds(start, size)],
            send_sem=send_sems.at[bits + step],
            recv_sem=recv_sems.at[bits + step],
            device_id=(tile, partner(bit)),
            device_id_type=pl.DeviceIdType.MESH,
        )
        copy.start()
        copy.wait()
        start = start - side * size
        size = 2 * size


def broadcast_from(value, axis, root):
    count = lax.axis_size(axis)
    assert count & (count - 1) == 0
    bits = count.bit_length() - 1
    planes = -(-value.shape[0] // count) * count
    padded = jnp.concatenate(
        [value, jnp.zeros((planes - value.shape[0],) + value.shape[1:], value.dtype)]
    )
    masked = jnp.where(lax.axis_index(axis) == root, padded, jnp.zeros_like(padded))
    vmem = pl.BlockSpec(memory_space=pltpu.VMEM)
    spread = pl.pallas_call(
        spread_kernel,
        out_shape=jax.ShapeDtypeStruct(padded.shape, padded.dtype),
        in_specs=[vmem],
        out_specs=vmem,
        scratch_shapes=[
            pltpu.VMEM((planes >> (bit + 1),) + value.shape[1:], value.dtype)
            for bit in range(bits)
        ]
        + [
            pltpu.SemaphoreType.DMA((2 * bits,)),
            pltpu.SemaphoreType.DMA((2 * bits,)),
            pltpu.SemaphoreType.REGULAR((bits,)),
        ],
        compiler_params=pltpu.CompilerParams(collective_id=0, has_side_effects=True),
    )(masked)
    return spread[: value.shape[0]]


def transport_kernel(
    scalars, own, south, north, courant, south_courant, north_courant, coefficient,
    emissions, out, held, pivots, ratios, lowers, planes,
):
    height, _, tracer_count, width = own.shape
    levels = held.shape[0]
    halo = south.shape[0]
    rows = height + 2 * halo
    level = pl.program_id(0)
    lane_shape = (tracer_count, width)

    def spread(row_ref, row):
        return jnp.broadcast_to(row_ref[pl.ds(row, 1), :], lane_shape)

    @pl.when(level == 0)
    def _prepare():
        zero_plane = jnp.zeros((height, width), jnp.float32)
        previous_ratio = zero_plane
        for lev in range(levels):
            lower_coef = coefficient[lev - 1] if lev > 0 else zero_plane
            upper_coef = coefficient[lev] if lev < levels - 1 else zero_plane
            pivot = 1.0 / (1.0 + lower_coef + upper_coef - lower_coef * previous_ratio)
            previous_ratio = upper_coef * pivot
            planes[0] = pivot
            planes[1] = previous_ratio
            planes[2] = lower_coef
            for row in range(height):
                pivots[lev, row] = spread(planes.at[0], row)
                ratios[lev, row] = spread(planes.at[1], row)
                lowers[lev, row] = spread(planes.at[2], row)

    def wind_row(component, row):
        index = component * levels + level
        if row < halo:
            return spread(south_courant.at[index], row)
        if row < halo + height:
            return spread(courant.at[index], row - halo)
        return spread(north_courant.at[index], row - halo - height)

    first_row = scalars[3 * ROUNDS]
    zonal_up, zonal_down, merid_up, merid_down = [], [], [], []
    for row in range(rows):
        zonal = wind_row(0, row)
        meridional = wind_row(1, row)
        if row == halo:
            meridional = meridional * first_row
        zonal_up.append(jnp.maximum(zonal, 0.0))
        zonal_down.append(jnp.minimum(zonal, 0.0))
        merid_up.append(jnp.maximum(meridional, 0.0))
        merid_down.append(jnp.minimum(meridional, 0.0))

    mixing = [south[row, 0] for row in range(halo)]
    mixing += [own[row, 0] for row in range(height)]
    mixing += [north[row, 0] for row in range(halo)]
    for substep in range(ROUNDS):
        low, high = substep + 1, rows - 2 - substep
        south_flux = {}
        for row in range(low, high + 2):
            south_flux[row] = merid_up[row] * mixing[row - 1] + merid_down[row] * mixing[row]
        advanced = list(mixing)
        for row in range(low, high + 1):
            band = 0 if row < halo else (1 if row < halo + height else 2)
            fraction = scalars[3 * substep + band]
            from_west = pltpu.roll(mixing[row], 1, 1)
            west_flux = zonal_up[row] * from_west + zonal_down[row] * mixing[row]
            east_flux = pltpu.roll(west_flux, width - 1, 1)
            advanced[row] = mixing[row] - fraction * (
                (east_flux - west_flux) + (south_flux[row + 1] - south_flux[row])
            )
        mixing = advanced
    for row in range(height):
        held[level, row] = mixing[halo + row]

    @pl.when(level == levels - 1)
    def _finish():
        for row in range(height):
            held[0, row] = held[0, row] + emissions[row]
            previous_value = jnp.zeros(lane_shape, jnp.float32)
            for lev in range(levels):
                previous_value = (
                    held[lev, row] + lowers[lev, row] * previous_value
                ) * pivots[lev, row]
                held[lev, row] = previous_value
            current = held[levels - 1, row]
            out[row, levels - 1] = current
            for lev in range(levels - 2, -1, -1):
                current = held[lev, row] + ratios[lev, row] * current
                out[row, lev] = current


def transport(scalars, own, south, north, courant, south_courant, north_courant,
              coefficient, emissions):
    height, levels, tracer_count, width = own.shape
    halo = south.shape[0]

    def whole(shape):
        return pl.BlockSpec(shape, lambda i: (0,) * len(shape))

    def by_level(shape):
        return pl.BlockSpec((shape[0], 1) + shape[2:], lambda i: (0, i, 0, 0))

    table = pltpu.VMEM((levels, height, tracer_count, width), jnp.float32)
    return pl.pallas_call(
        transport_kernel,
        grid=(levels,),
        out_shape=jax.ShapeDtypeStruct(own.shape, jnp.float32),
        in_specs=[
            pl.BlockSpec(memory_space=pltpu.SMEM),
            by_level(own.shape),
            by_level(south.shape),
            by_level(north.shape),
            whole(courant.shape),
            whole(south_courant.shape),
            whole(north_courant.shape),
            whole(coefficient.shape),
            whole(emissions.shape),
        ],
        out_specs=whole(own.shape),
        scratch_shapes=[
            table,
            table,
            table,
            table,
            pltpu.VMEM((3, height, width), jnp.float32),
        ],
        cost_estimate=pl.CostEstimate(
            flops=levels * tracer_count * width * 78 * 14,
            bytes_accessed=4 * (3 * own.size + 2 * south.size + 3 * courant.size),
            transcendentals=0,
        ),
    )(scalars, own, south, north, courant, south_courant, north_courant,
      coefficient, emissions)


def shards(tracers, emissions, winds, diffusivity, substeps, loader):
    tiles = lax.axis_size("tile")
    tile_position = lax.axis_index("tile")
    tile_numbers = jnp.arange(substeps.shape[0])
    loader_slot = jnp.sum(jnp.where(tile_numbers == tile_position, loader, 0))
    levels = tracers.shape[1]
    height = tracers.shape[2]
    width = tracers.shape[3]
    halo = ROUNDS

    local = jnp.concatenate(
        [winds[0].reshape(2 * levels, height, width), diffusivity[0]], axis=0
    )
    chosen = broadcast_from(local, "group", loader_slot)
    courant = chosen[: 2 * levels]
    coefficient = chosen[2 * levels :]

    by_row = jnp.transpose(tracers, (2, 1, 0, 3))
    south_rows = from_behind(by_row[height - halo :], "tile", 1)
    north_rows = from_behind(by_row[:halo], "tile", -1)
    south_courant = from_behind(courant[:, height - halo :], "tile", 1)
    north_courant = from_behind(courant[:, :halo], "tile", -1)

    def count_of(position):
        clamped = jnp.clip(position, 0, tiles - 1)
        return jnp.sum(jnp.where(tile_numbers == clamped, substeps, 0))

    counts = jnp.stack(
        [count_of(tile_position - 1), count_of(tile_position), count_of(tile_position + 1)]
    )
    counts_float = counts.astype(jnp.float32)
    steps = jnp.arange(ROUNDS)[:, None]
    fractions = jnp.where(steps < counts[None, :], 1.0 / counts_float[None, :], jnp.float32(0.0))
    first_row = jnp.where(tile_position > 0, jnp.float32(1.0), jnp.float32(0.0))
    scalars = jnp.concatenate([fractions.reshape(-1), first_row[None]])
    mixed = transport(
        scalars, by_row, south_rows, north_rows, courant, south_courant,
        north_courant, coefficient, jnp.transpose(emissions, (1, 0, 2)),
    )
    return jnp.transpose(mixed, (2, 1, 0, 3))


def solution(mesh):
    return jax.shard_map(
        shards,
        mesh=mesh,
        in_specs=(
            P("group", None, "tile", None),
            P("group", "tile", None),
            P("group", None, None, "tile", None),
            P("group", None, "tile", None),
            P(),
            P(),
        ),
        out_specs=P("group", None, "tile", None),
        check_vma=False,
    )
```

```python
import jax
import jax.numpy as jnp
from jax import lax
from jax.experimental import pallas as pl
from jax.experimental.pallas import tpu as pltpu
from jax.sharding import PartitionSpec as P

ROUNDS = 6


def from_behind(value, axis, by):
    count = lax.axis_size(axis)
    pairs = [(i, i + by) for i in range(count) if 0 <= i + by < count]
    return lax.ppermute(value, axis, pairs)


def broadcast_from(value, axis, root):
    count = lax.axis_size(axis)
    assert count & (count - 1) == 0 and count >= 2
    position = lax.axis_index(axis)
    distance = position ^ root
    core = position % 2
    half = -(-value.shape[0] // 2)
    padded = jnp.concatenate(
        [value, jnp.zeros((2 * half - value.shape[0],) + value.shape[1:], value.dtype)]
    )
    low, high = padded[:half], padded[half:]
    mine = jnp.where(core == 0, low, high)
    theirs = jnp.where(core == 0, high, low)

    def swap(current, bit):
        pairs = [(i, i ^ (1 << bit)) for i in range(count)]
        return lax.ppermute(current, axis, pairs)

    current = jnp.where(distance == 1, swap(theirs, 0), mine)
    bit = 1
    while (1 << bit) < count:
        current = jnp.where((distance >> bit) == 1, swap(current, bit), current)
        bit += 1
    other = swap(current, 0)
    whole = jnp.where(
        core == 0,
        jnp.concatenate([current, other]),
        jnp.concatenate([other, current]),
    )
    return whole[: value.shape[0]]


def transport_kernel(
    scalars, own, south, north, courant, south_courant, north_courant, coefficient,
    emissions, out, held, pivots, ratios, lowers, planes,
):
    height, _, tracer_count, width = own.shape
    levels = held.shape[0]
    halo = south.shape[0]
    rows = height + 2 * halo
    level = pl.program_id(0)
    lane_shape = (tracer_count, width)

    def spread(row_ref, row):
        return jnp.broadcast_to(row_ref[pl.ds(row, 1), :], lane_shape)

    @pl.when(level == 0)
    def _prepare():
        zero_plane = jnp.zeros((height, width), jnp.float32)
        previous_ratio = zero_plane
        for lev in range(levels):
            lower_coef = coefficient[lev - 1] if lev > 0 else zero_plane
            upper_coef = coefficient[lev] if lev < levels - 1 else zero_plane
            pivot = 1.0 / (1.0 + lower_coef + upper_coef - lower_coef * previous_ratio)
            previous_ratio = upper_coef * pivot
            planes[0] = pivot
            planes[1] = previous_ratio
            planes[2] = lower_coef
            for row in range(height):
                pivots[lev, row] = spread(planes.at[0], row)
                ratios[lev, row] = spread(planes.at[1], row)
                lowers[lev, row] = spread(planes.at[2], row)

    def wind_row(component, row):
        index = component * levels + level
        if row < halo:
            return spread(south_courant.at[index], row)
        if row < halo + height:
            return spread(courant.at[index], row - halo)
        return spread(north_courant.at[index], row - halo - height)

    first_row = scalars[3 * ROUNDS]
    zonal_up, zonal_down, merid_up, merid_down = [], [], [], []
    for row in range(rows):
        zonal = wind_row(0, row)
        meridional = wind_row(1, row)
        if row == halo:
            meridional = meridional * first_row
        zonal_up.append(jnp.maximum(zonal, 0.0))
        zonal_down.append(jnp.minimum(zonal, 0.0))
        merid_up.append(jnp.maximum(meridional, 0.0))
        merid_down.append(jnp.minimum(meridional, 0.0))

    mixing = [south[row, 0] for row in range(halo)]
    mixing += [own[row, 0] for row in range(height)]
    mixing += [north[row, 0] for row in range(halo)]
    for substep in range(ROUNDS):
        low, high = substep + 1, rows - 2 - substep
        south_flux = {}
        for row in range(low, high + 2):
            south_flux[row] = merid_up[row] * mixing[row - 1] + merid_down[row] * mixing[row]
        advanced = list(mixing)
        for row in range(low, high + 1):
            band = 0 if row < halo else (1 if row < halo + height else 2)
            fraction = scalars[3 * substep + band]
            from_west = pltpu.roll(mixing[row], 1, 1)
            west_flux = zonal_up[row] * from_west + zonal_down[row] * mixing[row]
            east_flux = pltpu.roll(west_flux, width - 1, 1)
            advanced[row] = mixing[row] - fraction * (
                (east_flux - west_flux) + (south_flux[row + 1] - south_flux[row])
            )
        mixing = advanced
    for row in range(height):
        held[level, row] = mixing[halo + row]

    @pl.when(level == levels - 1)
    def _finish():
        for row in range(height):
            held[0, row] = held[0, row] + emissions[row]
            previous_value = jnp.zeros(lane_shape, jnp.float32)
            for lev in range(levels):
                previous_value = (
                    held[lev, row] + lowers[lev, row] * previous_value
                ) * pivots[lev, row]
                held[lev, row] = previous_value
            current = held[levels - 1, row]
            out[row, levels - 1] = current
            for lev in range(levels - 2, -1, -1):
                current = held[lev, row] + ratios[lev, row] * current
                out[row, lev] = current


def transport(scalars, own, south, north, courant, south_courant, north_courant,
              coefficient, emissions):
    height, levels, tracer_count, width = own.shape
    halo = south.shape[0]

    def whole(shape):
        return pl.BlockSpec(shape, lambda i: (0,) * len(shape))

    def by_level(shape):
        return pl.BlockSpec((shape[0], 1) + shape[2:], lambda i: (0, i, 0, 0))

    table = pltpu.VMEM((levels, height, tracer_count, width), jnp.float32)
    return pl.pallas_call(
        transport_kernel,
        grid=(levels,),
        out_shape=jax.ShapeDtypeStruct(own.shape, jnp.float32),
        in_specs=[
            pl.BlockSpec(memory_space=pltpu.SMEM),
            by_level(own.shape),
            by_level(south.shape),
            by_level(north.shape),
            whole(courant.shape),
            whole(south_courant.shape),
            whole(north_courant.shape),
            whole(coefficient.shape),
            whole(emissions.shape),
        ],
        out_specs=whole(own.shape),
        scratch_shapes=[
            table,
            table,
            table,
            table,
            pltpu.VMEM((3, height, width), jnp.float32),
        ],
        cost_estimate=pl.CostEstimate(
            flops=levels * tracer_count * width * 78 * 14,
            bytes_accessed=4 * (3 * own.size + 2 * south.size + 3 * courant.size),
            transcendentals=0,
        ),
    )(scalars, own, south, north, courant, south_courant, north_courant,
      coefficient, emissions)


def shards(tracers, emissions, winds, diffusivity, substeps, loader):
    tiles = lax.axis_size("tile")
    tile_position = lax.axis_index("tile")
    tile_numbers = jnp.arange(substeps.shape[0])
    loader_slot = jnp.sum(jnp.where(tile_numbers == tile_position, loader, 0))
    levels = tracers.shape[1]
    height = tracers.shape[2]
    width = tracers.shape[3]
    halo = ROUNDS

    local = jnp.concatenate(
        [winds[0].reshape(2 * levels, height, width), diffusivity[0]], axis=0
    )
    chosen = broadcast_from(local, "group", loader_slot)
    courant = chosen[: 2 * levels]
    coefficient = chosen[2 * levels :]

    by_row = jnp.transpose(tracers, (2, 1, 0, 3))
    south_rows = from_behind(by_row[height - halo :], "tile", 1)
    north_rows = from_behind(by_row[:halo], "tile", -1)
    south_courant = from_behind(courant[:, height - halo :], "tile", 1)
    north_courant = from_behind(courant[:, :halo], "tile", -1)

    def count_of(position):
        clamped = jnp.clip(position, 0, tiles - 1)
        return jnp.sum(jnp.where(tile_numbers == clamped, substeps, 0))

    counts = jnp.stack(
        [count_of(tile_position - 1), count_of(tile_position), count_of(tile_position + 1)]
    )
    counts_float = counts.astype(jnp.float32)
    steps = jnp.arange(ROUNDS)[:, None]
    fractions = jnp.where(steps < counts[None, :], 1.0 / counts_float[None, :], jnp.float32(0.0))
    first_row = jnp.where(tile_position > 0, jnp.float32(1.0), jnp.float32(0.0))
    scalars = jnp.concatenate([fractions.reshape(-1), first_row[None]])
    mixed = transport(
        scalars, by_row, south_rows, north_rows, courant, south_courant,
        north_courant, coefficient, jnp.transpose(emissions, (1, 0, 2)),
    )
    return jnp.transpose(mixed, (2, 1, 0, 3))


def solution(mesh):
    return jax.shard_map(
        shards,
        mesh=mesh,
        in_specs=(
            P("group", None, "tile", None),
            P("group", "tile", None),
            P("group", None, None, "tile", None),
            P("group", None, "tile", None),
            P(),
            P(),
        ),
        out_specs=P("group", None, "tile", None),
        check_vma=False,
    )
```

```python
import jax
import jax.numpy as jnp
from jax import lax
from jax.experimental import pallas as pl
from jax.experimental.pallas import tpu as pltpu
from jax.sharding import PartitionSpec as P

ROUNDS = 6


def from_behind(value, axis, by):
    count = lax.axis_size(axis)
    pairs = [(i, i + by) for i in range(count) if 0 <= i + by < count]
    return lax.ppermute(value, axis, pairs)


def broadcast_from(value, axis, root):
    count = lax.axis_size(axis)
    assert count & (count - 1) == 0 and count >= 2
    position = lax.axis_index(axis)
    distance = position ^ root
    core = position % 2
    half = -(-value.shape[0] // 2)
    padded = jnp.concatenate(
        [value, jnp.zeros((2 * half - value.shape[0],) + value.shape[1:], value.dtype)]
    )
    low, high = padded[:half], padded[half:]
    mine = jnp.where(core == 0, low, high)
    theirs = jnp.where(core == 0, high, low)

    def swap(current, bit):
        pairs = [(i, i ^ (1 << bit)) for i in range(count)]
        return lax.ppermute(current, axis, pairs)

    current = jnp.where(distance == 1, swap(theirs, 0), mine)
    bit = 1
    while (1 << bit) < count:
        current = jnp.where((distance >> bit) == 1, swap(current, bit), current)
        bit += 1
    other = swap(current, 0)
    whole = jnp.where(
        core == 0,
        jnp.concatenate([current, other]),
        jnp.concatenate([other, current]),
    )
    return whole[: value.shape[0]]


def transport_kernel(
    scalars, own, south, north, courant, south_courant, north_courant, coefficient,
    emissions, out, held, pivots, ratios, lowers, planes,
):
    levels, height, tracer_count, width = held.shape
    halo = south.shape[0]
    rows = height + 2 * halo
    lane_shape = (tracer_count, width)

    def spread(row_ref, row):
        return jnp.broadcast_to(row_ref[pl.ds(row, 1), :], lane_shape)

    def _prepare():
        zero_plane = jnp.zeros((height, width), jnp.float32)
        previous_ratio = zero_plane
        for lev in range(levels):
            lower_coef = coefficient[lev - 1] if lev > 0 else zero_plane
            upper_coef = coefficient[lev] if lev < levels - 1 else zero_plane
            pivot = 1.0 / (1.0 + lower_coef + upper_coef - lower_coef * previous_ratio)
            previous_ratio = upper_coef * pivot
            planes[0] = pivot
            planes[1] = previous_ratio
            planes[2] = lower_coef
            for row in range(height):
                pivots[lev, row] = spread(planes.at[0], row)
                ratios[lev, row] = spread(planes.at[1], row)
                lowers[lev, row] = spread(planes.at[2], row)

    _prepare()

    def advect(level, carry):
        def wind_row(component, row):
            index = component * levels + level
            if row < halo:
                return spread(south_courant.at[index], row)
            if row < halo + height:
                return spread(courant.at[index], row - halo)
            return spread(north_courant.at[index], row - halo - height)

        first_row = scalars[3 * ROUNDS]
        zonal_up, zonal_down, merid_up, merid_down = [], [], [], []
        for row in range(rows):
            zonal = wind_row(0, row)
            meridional = wind_row(1, row)
            if row == halo:
                meridional = meridional * first_row
            zonal_up.append(jnp.maximum(zonal, 0.0))
            zonal_down.append(jnp.minimum(zonal, 0.0))
            merid_up.append(jnp.maximum(meridional, 0.0))
            merid_down.append(jnp.minimum(meridional, 0.0))

        mixing = [south[row, level] for row in range(halo)]
        mixing += [own[row, level] for row in range(height)]
        mixing += [north[row, level] for row in range(halo)]
        for substep in range(ROUNDS):
            low, high = substep + 1, rows - 2 - substep
            south_flux = {}
            for row in range(low, high + 2):
                south_flux[row] = merid_up[row] * mixing[row - 1] + merid_down[row] * mixing[row]
            advanced = list(mixing)
            for row in range(low, high + 1):
                band = 0 if row < halo else (1 if row < halo + height else 2)
                fraction = scalars[3 * substep + band]
                from_west = pltpu.roll(mixing[row], 1, 1)
                west_flux = zonal_up[row] * from_west + zonal_down[row] * mixing[row]
                east_flux = pltpu.roll(west_flux, width - 1, 1)
                advanced[row] = mixing[row] - fraction * (
                    (east_flux - west_flux) + (south_flux[row + 1] - south_flux[row])
                )
            mixing = advanced
        for row in range(height):
            held[level, row] = mixing[halo + row]
        return carry

    lax.fori_loop(0, levels, advect, 0)

    def _finish():
        for row in range(height):
            held[0, row] = held[0, row] + emissions[row]
            previous_value = jnp.zeros(lane_shape, jnp.float32)
            for lev in range(levels):
                previous_value = (
                    held[lev, row] + lowers[lev, row] * previous_value
                ) * pivots[lev, row]
                held[lev, row] = previous_value
            current = held[levels - 1, row]
            out[row, levels - 1] = current
            for lev in range(levels - 2, -1, -1):
                current = held[lev, row] + ratios[lev, row] * current
                out[row, lev] = current

    _finish()


def transport(scalars, own, south, north, courant, south_courant, north_courant,
              coefficient, emissions):
    height, levels, tracer_count, width = own.shape
    vmem = pl.BlockSpec(memory_space=pltpu.VMEM)
    table = pltpu.VMEM((levels, height, tracer_count, width), jnp.float32)
    return pl.pallas_call(
        transport_kernel,
        out_shape=jax.ShapeDtypeStruct(own.shape, jnp.float32),
        in_specs=[pl.BlockSpec(memory_space=pltpu.SMEM)] + [vmem] * 8,
        out_specs=vmem,
        scratch_shapes=[
            table,
            table,
            table,
            table,
            pltpu.VMEM((3, height, width), jnp.float32),
        ],
        cost_estimate=pl.CostEstimate(
            flops=levels * tracer_count * width * 78 * 14,
            bytes_accessed=4 * (2 * own.size + 2 * south.size + 3 * courant.size),
            transcendentals=0,
        ),
    )(scalars, own, south, north, courant, south_courant, north_courant,
      coefficient, emissions)


def shards(tracers, emissions, winds, diffusivity, substeps, loader):
    tiles = lax.axis_size("tile")
    tile_position = lax.axis_index("tile")
    tile_numbers = jnp.arange(substeps.shape[0])
    loader_slot = jnp.sum(jnp.where(tile_numbers == tile_position, loader, 0))
    levels = tracers.shape[1]
    height = tracers.shape[2]
    width = tracers.shape[3]
    halo = ROUNDS

    local = jnp.concatenate(
        [winds[0].reshape(2 * levels, height, width), diffusivity[0]], axis=0
    )
    chosen = broadcast_from(local, "group", loader_slot)
    courant = chosen[: 2 * levels]
    coefficient = chosen[2 * levels :]

    by_row = jnp.transpose(tracers, (2, 1, 0, 3))
    south_rows = from_behind(by_row[height - halo :], "tile", 1)
    north_rows = from_behind(by_row[:halo], "tile", -1)
    south_courant = from_behind(courant[:, height - halo :], "tile", 1)
    north_courant = from_behind(courant[:, :halo], "tile", -1)

    def count_of(position):
        clamped = jnp.clip(position, 0, tiles - 1)
        return jnp.sum(jnp.where(tile_numbers == clamped, substeps, 0))

    counts = jnp.stack(
        [count_of(tile_position - 1), count_of(tile_position), count_of(tile_position + 1)]
    )
    counts_float = counts.astype(jnp.float32)
    steps = jnp.arange(ROUNDS)[:, None]
    fractions = jnp.where(steps < counts[None, :], 1.0 / counts_float[None, :], jnp.float32(0.0))
    first_row = jnp.where(tile_position > 0, jnp.float32(1.0), jnp.float32(0.0))
    scalars = jnp.concatenate([fractions.reshape(-1), first_row[None]])
    mixed = transport(
        scalars, by_row, south_rows, north_rows, courant, south_courant,
        north_courant, coefficient, jnp.transpose(emissions, (1, 0, 2)),
    )
    return jnp.transpose(mixed, (2, 1, 0, 3))


def solution(mesh):
    return jax.shard_map(
        shards,
        mesh=mesh,
        in_specs=(
            P("group", None, "tile", None),
            P("group", "tile", None),
            P("group", None, None, "tile", None),
            P("group", None, "tile", None),
            P(),
            P(),
        ),
        out_specs=P("group", None, "tile", None),
        check_vma=False,
    )
```

```python
import jax
import jax.numpy as jnp
from jax import lax
from jax.experimental import pallas as pl
from jax.experimental.pallas import tpu as pltpu
from jax.sharding import PartitionSpec as P

ROUNDS = 6


def from_behind(value, axis, by):
    count = lax.axis_size(axis)
    pairs = [(i, i + by) for i in range(count) if 0 <= i + by < count]
    return lax.ppermute(value, axis, pairs)


def broadcast_from(value, axis, root):
    count = lax.axis_size(axis)
    assert count & (count - 1) == 0 and count >= 2
    position = lax.axis_index(axis)
    distance = position ^ root
    core = position % 2
    half = -(-value.shape[0] // 2)
    padded = jnp.concatenate(
        [value, jnp.zeros((2 * half - value.shape[0],) + value.shape[1:], value.dtype)]
    )
    low, high = padded[:half], padded[half:]
    mine = jnp.where(core == 0, low, high)
    theirs = jnp.where(core == 0, high, low)

    def swap(current, bit):
        pairs = [(i, i ^ (1 << bit)) for i in range(count)]
        return lax.ppermute(current, axis, pairs)

    current = jnp.where(distance == 1, swap(theirs, 0), mine)
    bit = 1
    while (1 << bit) < count:
        current = jnp.where((distance >> bit) == 1, swap(current, bit), current)
        bit += 1
    other = swap(current, 0)
    whole = jnp.where(
        core == 0,
        jnp.concatenate([current, other]),
        jnp.concatenate([other, current]),
    )
    return whole


def transport_kernel(
    substeps, own, south, north, chosen, south_courant, north_courant, emissions, out,
    held, pivots, ratios, lowers, planes, fractions,
):
    levels, height, tracer_count, width = held.shape
    halo = south.shape[0]
    rows = height + 2 * halo
    lane_shape = (tracer_count, width)

    def spread(row_ref, row):
        return jnp.broadcast_to(row_ref[pl.ds(row, 1), :], lane_shape)

    tiles = substeps.shape[0]
    tile_position = lax.axis_index("tile")
    courant = chosen
    coefficient = chosen.at[pl.ds(2 * levels, levels - 1)]

    def _prepare():
        bands = (
            jnp.maximum(tile_position - 1, 0),
            tile_position,
            jnp.minimum(tile_position + 1, tiles - 1),
        )
        for band, position in enumerate(bands):
            count = substeps[position]
            spread_count = jnp.full(lane_shape, count.astype(jnp.float32))
            for substep in range(ROUNDS):
                fractions[3 * substep + band] = jnp.where(
                    substep < count, 1.0 / spread_count, jnp.float32(0.0)
                )
        zero_plane = jnp.zeros((height, width), jnp.float32)
        previous_ratio = zero_plane
        for lev in range(levels):
            lower_coef = coefficient[lev - 1] if lev > 0 else zero_plane
            upper_coef = coefficient[lev] if lev < levels - 1 else zero_plane
            pivot = 1.0 / (1.0 + lower_coef + upper_coef - lower_coef * previous_ratio)
            previous_ratio = upper_coef * pivot
            planes[0] = pivot
            planes[1] = previous_ratio
            planes[2] = lower_coef
            for row in range(height):
                pivots[lev, row] = spread(planes.at[0], row)
                ratios[lev, row] = spread(planes.at[1], row)
                lowers[lev, row] = spread(planes.at[2], row)

    _prepare()

    def advect(level, carry):
        def wind_row(component, row):
            index = component * levels + level
            if row < halo:
                return spread(south_courant.at[index], row)
            if row < halo + height:
                return spread(courant.at[index], row - halo)
            return spread(north_courant.at[index], row - halo - height)

        first_row = jnp.where(tile_position > 0, jnp.float32(1.0), jnp.float32(0.0))
        zonal_up, zonal_down, merid_up, merid_down = [], [], [], []
        for row in range(rows):
            zonal = wind_row(0, row)
            meridional = wind_row(1, row)
            if row == halo:
                meridional = meridional * first_row
            zonal_up.append(jnp.maximum(zonal, 0.0))
            zonal_down.append(jnp.minimum(zonal, 0.0))
            merid_up.append(jnp.maximum(meridional, 0.0))
            merid_down.append(jnp.minimum(meridional, 0.0))

        mixing = [south[row, level] for row in range(halo)]
        mixing += [own[row, level] for row in range(height)]
        mixing += [north[row, level] for row in range(halo)]
        for substep in range(ROUNDS):
            low, high = substep + 1, rows - 2 - substep
            south_flux = {}
            for row in range(low, high + 2):
                south_flux[row] = merid_up[row] * mixing[row - 1] + merid_down[row] * mixing[row]
            advanced = list(mixing)
            for row in range(low, high + 1):
                band = 0 if row < halo else (1 if row < halo + height else 2)
                fraction = fractions[3 * substep + band]
                from_west = pltpu.roll(mixing[row], 1, 1)
                west_flux = zonal_up[row] * from_west + zonal_down[row] * mixing[row]
                east_flux = pltpu.roll(west_flux, width - 1, 1)
                advanced[row] = mixing[row] - fraction * (
                    (east_flux - west_flux) + (south_flux[row + 1] - south_flux[row])
                )
            mixing = advanced
        for row in range(height):
            held[level, row] = mixing[halo + row]
        return carry

    lax.fori_loop(0, levels, advect, 0)

    def _finish():
        for row in range(height):
            held[0, row] = held[0, row] + emissions[row]
            previous_value = jnp.zeros(lane_shape, jnp.float32)
            for lev in range(levels):
                previous_value = (
                    held[lev, row] + lowers[lev, row] * previous_value
                ) * pivots[lev, row]
                held[lev, row] = previous_value
            current = held[levels - 1, row]
            out[row, levels - 1] = current
            for lev in range(levels - 2, -1, -1):
                current = held[lev, row] + ratios[lev, row] * current
                out[row, lev] = current

    _finish()


def transport(substeps, own, south, north, chosen, south_courant, north_courant,
              emissions):
    height, levels, tracer_count, width = own.shape
    vmem = pl.BlockSpec(memory_space=pltpu.VMEM)
    table = pltpu.VMEM((levels, height, tracer_count, width), jnp.float32)
    return pl.pallas_call(
        transport_kernel,
        out_shape=jax.ShapeDtypeStruct(own.shape, jnp.float32),
        in_specs=[pl.BlockSpec(memory_space=pltpu.SMEM)] + [vmem] * 7,
        out_specs=vmem,
        scratch_shapes=[
            table,
            table,
            table,
            table,
            pltpu.VMEM((3, height, width), jnp.float32),
            pltpu.VMEM((3 * ROUNDS, tracer_count, width), jnp.float32),
        ],
        cost_estimate=pl.CostEstimate(
            flops=levels * tracer_count * width * 78 * 14,
            bytes_accessed=4 * (2 * own.size + 2 * south.size + chosen.size),
            transcendentals=0,
        ),
    )(substeps, own, south, north, chosen, south_courant, north_courant, emissions)


def shards(tracers, emissions, winds, diffusivity, substeps, loader):
    tiles = lax.axis_size("tile")
    tile_position = lax.axis_index("tile")
    tile_numbers = jnp.arange(substeps.shape[0])
    loader_slot = jnp.sum(jnp.where(tile_numbers == tile_position, loader, 0))
    levels = tracers.shape[1]
    height = tracers.shape[2]
    width = tracers.shape[3]
    halo = ROUNDS

    local = jnp.concatenate(
        [winds[0].reshape(2 * levels, height, width), diffusivity[0]], axis=0
    )
    chosen = broadcast_from(local, "group", loader_slot)
    courant = chosen[: 2 * levels]

    by_row = jnp.transpose(tracers, (2, 1, 0, 3))
    south_rows = from_behind(by_row[height - halo :], "tile", 1)
    north_rows = from_behind(by_row[:halo], "tile", -1)
    south_courant = from_behind(courant[:, height - halo :], "tile", 1)
    north_courant = from_behind(courant[:, :halo], "tile", -1)
    mixed = transport(
        substeps, by_row, south_rows, north_rows, chosen, south_courant,
        north_courant, jnp.transpose(emissions, (1, 0, 2)),
    )
    return jnp.transpose(mixed, (2, 1, 0, 3))


def solution(mesh):
    return jax.shard_map(
        shards,
        mesh=mesh,
        in_specs=(
            P("group", None, "tile", None),
            P("group", "tile", None),
            P("group", None, None, "tile", None),
            P("group", None, "tile", None),
            P(),
            P(),
        ),
        out_specs=P("group", None, "tile", None),
        check_vma=False,
    )
```

```python
import jax
import jax.numpy as jnp
from jax import lax
from jax.experimental import pallas as pl
from jax.experimental.pallas import tpu as pltpu
from jax.sharding import PartitionSpec as P

ROUNDS = 6


def from_behind(value, axis, by):
    count = lax.axis_size(axis)
    pairs = [(i, i + by) for i in range(count) if 0 <= i + by < count]
    return lax.ppermute(value, axis, pairs)


def exchange_kernel(
    masked, up, down, chosen, south, north, south_courant, north_courant,
    total, received, send_sems, recv_sems,
):
    mesh = pl.DeviceIdType.MESH
    tiles = lax.axis_size("tile")
    bits = lax.axis_size("group").bit_length() - 1
    tile = lax.axis_index("tile")
    me = lax.axis_index("group")
    core = me % 2
    half = masked.shape[0] // 2
    planes = south_courant.shape[0]

    def partner(bit):
        return me + (1 << bit) * (1 - 2 * ((me // (1 << bit)) % 2))

    barrier = pltpu.get_barrier_semaphore()
    for bit in range(bits):
        pl.semaphore_signal(barrier, 1, device_id=(tile, partner(bit)), device_id_type=mesh)

    @pl.when(tile > 0)
    def _():
        pl.semaphore_signal(barrier, 1, device_id=(tile - 1, me), device_id_type=mesh)

    @pl.when(tile < tiles - 1)
    def _():
        pl.semaphore_signal(barrier, 1, device_id=(tile + 1, me), device_id_type=mesh)

    has_south = (tile + tiles - 1) // tiles
    has_north = (2 * tiles - 3 - tile) // (tiles - 1)
    pl.semaphore_wait(barrier, bits + has_south + has_north)

    def along_tile(source, target, slot, by):
        return pltpu.make_async_remote_copy(
            src_ref=source, dst_ref=target, send_sem=send_sems.at[slot],
            recv_sem=recv_sems.at[slot], device_id=(tile + by, me), device_id_type=mesh,
        )

    @pl.when(tile < tiles - 1)
    def _():
        along_tile(up, south, 0, 1).start()

    @pl.when(tile > 0)
    def _():
        along_tile(down, north, 1, -1).start()

    @pl.when(tile == 0)
    def _():
        south[...] = jnp.zeros_like(south)
        south_courant[...] = jnp.zeros_like(south_courant)

    @pl.when(tile == tiles - 1)
    def _():
        north[...] = jnp.zeros_like(north)
        north_courant[...] = jnp.zeros_like(north_courant)

    def along_group(source, bit, slot):
        copy = pltpu.make_async_remote_copy(
            src_ref=source, dst_ref=received.at[slot], send_sem=send_sems.at[2 + slot],
            recv_sem=recv_sems.at[2 + slot], device_id=(tile, partner(bit)),
            device_id_type=mesh,
        )
        copy.start()
        copy.wait()

    along_group(masked.at[pl.ds((1 - core) * half, half)], 0, 0)
    total[...] = masked[pl.ds(core * half, half)] + received[0]
    for bit in range(1, bits):
        along_group(total, bit, bit)
        total[...] = total[...] + received[bit]
    along_group(total, 0, bits)
    chosen[pl.ds(core * half, half)] = total[...]
    chosen[pl.ds((1 - core) * half, half)] = received[bits]

    @pl.when(tile < tiles - 1)
    def _():
        along_tile(chosen.at[pl.ds(0, planes)], south_courant, 2 + bits + 1, 1).start()

    @pl.when(tile > 0)
    def _():
        along_tile(chosen.at[pl.ds(0, planes)], north_courant, 2 + bits + 2, -1).start()

    @pl.when(tile < tiles - 1)
    def _():
        along_tile(up, south, 0, 1).wait_send()
        along_tile(chosen.at[pl.ds(0, planes)], south_courant, 2 + bits + 1, 1).wait_send()
        along_tile(up, north, 1, 1).wait_recv()
        along_tile(chosen.at[pl.ds(0, planes)], north_courant, 2 + bits + 2, 1).wait_recv()

    @pl.when(tile > 0)
    def _():
        along_tile(down, north, 1, -1).wait_send()
        along_tile(chosen.at[pl.ds(0, planes)], north_courant, 2 + bits + 2, -1).wait_send()
        along_tile(down, south, 0, -1).wait_recv()
        along_tile(chosen.at[pl.ds(0, planes)], south_courant, 2 + bits + 1, -1).wait_recv()


def exchange(value, by_row, root, halo, planes):
    groups = lax.axis_size("group")
    assert groups & (groups - 1) == 0 and groups >= 2
    bits = groups.bit_length() - 1
    half = -(-value.shape[0] // 2)
    padded = jnp.concatenate(
        [value, jnp.zeros((2 * half - value.shape[0],) + value.shape[1:], value.dtype)]
    )
    masked = jnp.where(lax.axis_index("group") == root, padded, jnp.zeros_like(padded))
    height = by_row.shape[0]
    vmem = pl.BlockSpec(memory_space=pltpu.VMEM)
    rows = jax.ShapeDtypeStruct((halo,) + by_row.shape[1:], by_row.dtype)
    winds = jax.ShapeDtypeStruct((planes,) + value.shape[1:], value.dtype)
    return pl.pallas_call(
        exchange_kernel,
        out_shape=(jax.ShapeDtypeStruct(padded.shape, padded.dtype), rows, rows, winds, winds),
        in_specs=[vmem] * 3,
        out_specs=(vmem,) * 5,
        scratch_shapes=[
            pltpu.VMEM((half,) + value.shape[1:], value.dtype),
            pltpu.VMEM((bits + 1, half) + value.shape[1:], value.dtype),
            pltpu.SemaphoreType.DMA((bits + 5,)),
            pltpu.SemaphoreType.DMA((bits + 5,)),
        ],
        compiler_params=pltpu.CompilerParams(collective_id=0, has_side_effects=True),
    )(masked, by_row[height - halo :], by_row[:halo])


def transport_kernel(
    substeps, own, south, north, chosen, south_courant, north_courant, emissions, out,
    held, pivots, ratios, lowers, planes, fractions,
):
    levels, height, tracer_count, width = held.shape
    halo = south.shape[0]
    rows = height + 2 * halo
    lane_shape = (tracer_count, width)

    def spread(row_ref, row):
        return jnp.broadcast_to(row_ref[pl.ds(row, 1), :], lane_shape)

    tiles = substeps.shape[0]
    tile_position = lax.axis_index("tile")
    courant = chosen
    coefficient = chosen.at[pl.ds(2 * levels, levels - 1)]

    def _prepare():
        bands = (
            jnp.maximum(tile_position - 1, 0),
            tile_position,
            jnp.minimum(tile_position + 1, tiles - 1),
        )
        for band, position in enumerate(bands):
            count = substeps[position]
            spread_count = jnp.full(lane_shape, count.astype(jnp.float32))
            for substep in range(ROUNDS):
                fractions[3 * substep + band] = jnp.where(
                    substep < count, 1.0 / spread_count, jnp.float32(0.0)
                )
        zero_plane = jnp.zeros((height, width), jnp.float32)
        previous_ratio = zero_plane
        for lev in range(levels):
            lower_coef = coefficient[lev - 1] if lev > 0 else zero_plane
            upper_coef = coefficient[lev] if lev < levels - 1 else zero_plane
            pivot = 1.0 / (1.0 + lower_coef + upper_coef - lower_coef * previous_ratio)
            previous_ratio = upper_coef * pivot
            planes[0] = pivot
            planes[1] = previous_ratio
            planes[2] = lower_coef
            for row in range(height):
                pivots[lev, row] = spread(planes.at[0], row)
                ratios[lev, row] = spread(planes.at[1], row)
                lowers[lev, row] = spread(planes.at[2], row)

    _prepare()

    def advect(level, carry):
        def wind_row(component, row):
            index = component * levels + level
            if row < halo:
                return spread(south_courant.at[index], row + height - halo)
            if row < halo + height:
                return spread(courant.at[index], row - halo)
            return spread(north_courant.at[index], row - halo - height)

        first_row = jnp.where(tile_position > 0, jnp.float32(1.0), jnp.float32(0.0))
        zonal_up, zonal_down, merid_up, merid_down = [], [], [], []
        for row in range(rows):
            zonal = wind_row(0, row)
            meridional = wind_row(1, row)
            if row == halo:
                meridional = meridional * first_row
            zonal_up.append(jnp.maximum(zonal, 0.0))
            zonal_down.append(jnp.minimum(zonal, 0.0))
            merid_up.append(jnp.maximum(meridional, 0.0))
            merid_down.append(jnp.minimum(meridional, 0.0))

        mixing = [south[row, level] for row in range(halo)]
        mixing += [own[row, level] for row in range(height)]
        mixing += [north[row, level] for row in range(halo)]
        for substep in range(ROUNDS):
            low, high = substep + 1, rows - 2 - substep
            south_flux = {}
            for row in range(low, high + 2):
                south_flux[row] = merid_up[row] * mixing[row - 1] + merid_down[row] * mixing[row]
            advanced = list(mixing)
            for row in range(low, high + 1):
                band = 0 if row < halo else (1 if row < halo + height else 2)
                fraction = fractions[3 * substep + band]
                from_west = pltpu.roll(mixing[row], 1, 1)
                west_flux = zonal_up[row] * from_west + zonal_down[row] * mixing[row]
                east_flux = pltpu.roll(west_flux, width - 1, 1)
                advanced[row] = mixing[row] - fraction * (
                    (east_flux - west_flux) + (south_flux[row + 1] - south_flux[row])
                )
            mixing = advanced
        for row in range(height):
            held[level, row] = mixing[halo + row]
        return carry

    lax.fori_loop(0, levels, advect, 0)

    def _finish():
        for row in range(height):
            held[0, row] = held[0, row] + emissions[row]
            previous_value = jnp.zeros(lane_shape, jnp.float32)
            for lev in range(levels):
                previous_value = (
                    held[lev, row] + lowers[lev, row] * previous_value
                ) * pivots[lev, row]
                held[lev, row] = previous_value
            current = held[levels - 1, row]
            out[row, levels - 1] = current
            for lev in range(levels - 2, -1, -1):
                current = held[lev, row] + ratios[lev, row] * current
                out[row, lev] = current

    _finish()


def transport(substeps, own, south, north, chosen, south_courant, north_courant,
              emissions):
    height, levels, tracer_count, width = own.shape
    vmem = pl.BlockSpec(memory_space=pltpu.VMEM)
    table = pltpu.VMEM((levels, height, tracer_count, width), jnp.float32)
    return pl.pallas_call(
        transport_kernel,
        out_shape=jax.ShapeDtypeStruct(own.shape, jnp.float32),
        in_specs=[pl.BlockSpec(memory_space=pltpu.SMEM)] + [vmem] * 7,
        out_specs=vmem,
        scratch_shapes=[
            table,
            table,
            table,
            table,
            pltpu.VMEM((3, height, width), jnp.float32),
            pltpu.VMEM((3 * ROUNDS, tracer_count, width), jnp.float32),
        ],
        cost_estimate=pl.CostEstimate(
            flops=levels * tracer_count * width * 78 * 14,
            bytes_accessed=4 * (2 * own.size + 2 * south.size + chosen.size),
            transcendentals=0,
        ),
    )(substeps, own, south, north, chosen, south_courant, north_courant, emissions)


def shards(tracers, emissions, winds, diffusivity, substeps, loader):
    tiles = lax.axis_size("tile")
    tile_position = lax.axis_index("tile")
    tile_numbers = jnp.arange(substeps.shape[0])
    loader_slot = jnp.sum(jnp.where(tile_numbers == tile_position, loader, 0))
    levels = tracers.shape[1]
    height = tracers.shape[2]
    width = tracers.shape[3]
    halo = ROUNDS

    local = jnp.concatenate(
        [winds[0].reshape(2 * levels, height, width), diffusivity[0]], axis=0
    )
    by_row = jnp.transpose(tracers, (2, 1, 0, 3))
    chosen, south_rows, north_rows, south_courant, north_courant = exchange(
        local, by_row, loader_slot, halo, 2 * levels
    )
    mixed = transport(
        substeps, by_row, south_rows, north_rows, chosen, south_courant,
        north_courant, jnp.transpose(emissions, (1, 0, 2)),
    )
    return jnp.transpose(mixed, (2, 1, 0, 3))


def solution(mesh):
    return jax.shard_map(
        shards,
        mesh=mesh,
        in_specs=(
            P("group", None, "tile", None),
            P("group", "tile", None),
            P("group", None, None, "tile", None),
            P("group", None, "tile", None),
            P(),
            P(),
        ),
        out_specs=P("group", None, "tile", None),
        check_vma=False,
    )
```

```python
import jax
import jax.numpy as jnp
from jax import lax
from jax.experimental import pallas as pl
from jax.experimental.pallas import tpu as pltpu
from jax.sharding import PartitionSpec as P

ROUNDS = 6


def from_behind(value, axis, by):
    count = lax.axis_size(axis)
    pairs = [(i, i + by) for i in range(count) if 0 <= i + by < count]
    return lax.ppermute(value, axis, pairs)


def exchange_kernel(
    masked, up, down, chosen, south, north, south_courant, north_courant,
    total, received, send_sems, recv_sems,
):
    mesh = pl.DeviceIdType.MESH
    tiles = lax.axis_size("tile")
    bits = lax.axis_size("group").bit_length() - 1
    tile = lax.axis_index("tile")
    me = lax.axis_index("group")
    core = me % 2
    half = masked.shape[0] // 2
    planes = south_courant.shape[0]

    def partner(bit):
        return me + (1 << bit) * (1 - 2 * ((me // (1 << bit)) % 2))

    barrier = pltpu.get_barrier_semaphore()
    for bit in range(bits):
        pl.semaphore_signal(barrier, 1, device_id=(tile, partner(bit)), device_id_type=mesh)

    @pl.when(tile > 0)
    def _():
        pl.semaphore_signal(barrier, 1, device_id=(tile - 1, me), device_id_type=mesh)

    @pl.when(tile < tiles - 1)
    def _():
        pl.semaphore_signal(barrier, 1, device_id=(tile + 1, me), device_id_type=mesh)

    has_south = (tile + tiles - 1) // tiles
    has_north = (2 * tiles - 3 - tile) // (tiles - 1)
    pl.semaphore_wait(barrier, bits + has_south + has_north)

    def along_tile(source, target, slot, by):
        return pltpu.make_async_remote_copy(
            src_ref=source, dst_ref=target, send_sem=send_sems.at[slot],
            recv_sem=recv_sems.at[slot], device_id=(tile + by, me), device_id_type=mesh,
        )

    @pl.when(tile == 0)
    def _():
        south[...] = jnp.zeros_like(south)
        south_courant[...] = jnp.zeros_like(south_courant)

    @pl.when(tile == tiles - 1)
    def _():
        north[...] = jnp.zeros_like(north)
        north_courant[...] = jnp.zeros_like(north_courant)

    def along_group(source, bit, slot):
        copy = pltpu.make_async_remote_copy(
            src_ref=source, dst_ref=received.at[slot], send_sem=send_sems.at[2 + slot],
            recv_sem=recv_sems.at[2 + slot], device_id=(tile, partner(bit)),
            device_id_type=mesh,
        )
        copy.start()
        copy.wait()

    along_group(masked.at[pl.ds((1 - core) * half, half)], 0, 0)
    total[...] = masked[pl.ds(core * half, half)] + received[0]
    for bit in range(1, bits):
        along_group(total, bit, bit)
        total[...] = total[...] + received[bit]
        if bit == 1:
            @pl.when(tile < tiles - 1)
            def _():
                along_tile(up, south, 0, 1).start()

            @pl.when(tile > 0)
            def _():
                along_tile(down, north, 1, -1).start()
    along_group(total, 0, bits)
    chosen[pl.ds(core * half, half)] = total[...]
    chosen[pl.ds((1 - core) * half, half)] = received[bits]

    @pl.when(tile < tiles - 1)
    def _():
        along_tile(chosen.at[pl.ds(0, planes)], south_courant, 2 + bits + 1, 1).start()

    @pl.when(tile > 0)
    def _():
        along_tile(chosen.at[pl.ds(0, planes)], north_courant, 2 + bits + 2, -1).start()

    @pl.when(tile < tiles - 1)
    def _():
        along_tile(up, south, 0, 1).wait_send()
        along_tile(chosen.at[pl.ds(0, planes)], south_courant, 2 + bits + 1, 1).wait_send()
        along_tile(up, north, 1, 1).wait_recv()
        along_tile(chosen.at[pl.ds(0, planes)], north_courant, 2 + bits + 2, 1).wait_recv()

    @pl.when(tile > 0)
    def _():
        along_tile(down, north, 1, -1).wait_send()
        along_tile(chosen.at[pl.ds(0, planes)], north_courant, 2 + bits + 2, -1).wait_send()
        along_tile(down, south, 0, -1).wait_recv()
        along_tile(chosen.at[pl.ds(0, planes)], south_courant, 2 + bits + 1, -1).wait_recv()


def exchange(value, by_row, root, halo, planes):
    groups = lax.axis_size("group")
    assert groups & (groups - 1) == 0 and groups >= 2
    bits = groups.bit_length() - 1
    half = -(-value.shape[0] // 2)
    padded = jnp.concatenate(
        [value, jnp.zeros((2 * half - value.shape[0],) + value.shape[1:], value.dtype)]
    )
    masked = jnp.where(lax.axis_index("group") == root, padded, jnp.zeros_like(padded))
    height = by_row.shape[0]
    vmem = pl.BlockSpec(memory_space=pltpu.VMEM)
    rows = jax.ShapeDtypeStruct((halo,) + by_row.shape[1:], by_row.dtype)
    winds = jax.ShapeDtypeStruct((planes,) + value.shape[1:], value.dtype)
    return pl.pallas_call(
        exchange_kernel,
        out_shape=(jax.ShapeDtypeStruct(padded.shape, padded.dtype), rows, rows, winds, winds),
        in_specs=[vmem] * 3,
        out_specs=(vmem,) * 5,
        scratch_shapes=[
            pltpu.VMEM((half,) + value.shape[1:], value.dtype),
            pltpu.VMEM((bits + 1, half) + value.shape[1:], value.dtype),
            pltpu.SemaphoreType.DMA((bits + 5,)),
            pltpu.SemaphoreType.DMA((bits + 5,)),
        ],
        compiler_params=pltpu.CompilerParams(collective_id=0, has_side_effects=True),
    )(masked, by_row[height - halo :], by_row[:halo])


def transport_kernel(
    substeps, own, south, north, chosen, south_courant, north_courant, emissions, out,
    held, pivots, ratios, lowers, planes, fractions,
):
    levels, height, tracer_count, width = held.shape
    halo = south.shape[0]
    rows = height + 2 * halo
    lane_shape = (tracer_count, width)

    def spread(row_ref, row):
        return jnp.broadcast_to(row_ref[pl.ds(row, 1), :], lane_shape)

    tiles = substeps.shape[0]
    tile_position = lax.axis_index("tile")
    courant = chosen
    coefficient = chosen.at[pl.ds(2 * levels, levels - 1)]

    def _prepare():
        bands = (
            jnp.maximum(tile_position - 1, 0),
            tile_position,
            jnp.minimum(tile_position + 1, tiles - 1),
        )
        for band, position in enumerate(bands):
            count = substeps[position]
            spread_count = jnp.full(lane_shape, count.astype(jnp.float32))
            for substep in range(ROUNDS):
                fractions[3 * substep + band] = jnp.where(
                    substep < count, 1.0 / spread_count, jnp.float32(0.0)
                )
        zero_plane = jnp.zeros((height, width), jnp.float32)
        previous_ratio = zero_plane
        for lev in range(levels):
            lower_coef = coefficient[lev - 1] if lev > 0 else zero_plane
            upper_coef = coefficient[lev] if lev < levels - 1 else zero_plane
            pivot = 1.0 / (1.0 + lower_coef + upper_coef - lower_coef * previous_ratio)
            previous_ratio = upper_coef * pivot
            planes[0] = pivot
            planes[1] = previous_ratio
            planes[2] = lower_coef
            for row in range(height):
                pivots[lev, row] = spread(planes.at[0], row)
                ratios[lev, row] = spread(planes.at[1], row)
                lowers[lev, row] = spread(planes.at[2], row)

    _prepare()

    def advect(level, carry):
        def wind_row(component, row):
            index = component * levels + level
            if row < halo:
                return spread(south_courant.at[index], row + height - halo)
            if row < halo + height:
                return spread(courant.at[index], row - halo)
            return spread(north_courant.at[index], row - halo - height)

        first_row = jnp.where(tile_position > 0, jnp.float32(1.0), jnp.float32(0.0))
        zonal_up, zonal_down, merid_up, merid_down = [], [], [], []
        for row in range(rows):
            zonal = wind_row(0, row)
            meridional = wind_row(1, row)
            if row == halo:
                meridional = meridional * first_row
            zonal_up.append(jnp.maximum(zonal, 0.0))
            zonal_down.append(jnp.minimum(zonal, 0.0))
            merid_up.append(jnp.maximum(meridional, 0.0))
            merid_down.append(jnp.minimum(meridional, 0.0))

        mixing = [south[row, level] for row in range(halo)]
        mixing += [own[row, level] for row in range(height)]
        mixing += [north[row, level] for row in range(halo)]
        for substep in range(ROUNDS):
            low, high = substep + 1, rows - 2 - substep
            south_flux = {}
            for row in range(low, high + 2):
                south_flux[row] = merid_up[row] * mixing[row - 1] + merid_down[row] * mixing[row]
            advanced = list(mixing)
            for row in range(low, high + 1):
                band = 0 if row < halo else (1 if row < halo + height else 2)
                fraction = fractions[3 * substep + band]
                from_west = pltpu.roll(mixing[row], 1, 1)
                west_flux = zonal_up[row] * from_west + zonal_down[row] * mixing[row]
                east_flux = pltpu.roll(west_flux, width - 1, 1)
                advanced[row] = mixing[row] - fraction * (
                    (east_flux - west_flux) + (south_flux[row + 1] - south_flux[row])
                )
            mixing = advanced
        for row in range(height):
            held[level, row] = mixing[halo + row]
        return carry

    lax.fori_loop(0, levels, advect, 0)

    def _finish():
        for row in range(height):
            held[0, row] = held[0, row] + emissions[row]
            previous_value = jnp.zeros(lane_shape, jnp.float32)
            for lev in range(levels):
                previous_value = (
                    held[lev, row] + lowers[lev, row] * previous_value
                ) * pivots[lev, row]
                held[lev, row] = previous_value
            current = held[levels - 1, row]
            out[row, levels - 1] = current
            for lev in range(levels - 2, -1, -1):
                current = held[lev, row] + ratios[lev, row] * current
                out[row, lev] = current

    _finish()


def transport(substeps, own, south, north, chosen, south_courant, north_courant,
              emissions):
    height, levels, tracer_count, width = own.shape
    vmem = pl.BlockSpec(memory_space=pltpu.VMEM)
    table = pltpu.VMEM((levels, height, tracer_count, width), jnp.float32)
    return pl.pallas_call(
        transport_kernel,
        out_shape=jax.ShapeDtypeStruct(own.shape, jnp.float32),
        in_specs=[pl.BlockSpec(memory_space=pltpu.SMEM)] + [vmem] * 7,
        out_specs=vmem,
        scratch_shapes=[
            table,
            table,
            table,
            table,
            pltpu.VMEM((3, height, width), jnp.float32),
            pltpu.VMEM((3 * ROUNDS, tracer_count, width), jnp.float32),
        ],
        cost_estimate=pl.CostEstimate(
            flops=levels * tracer_count * width * 78 * 14,
            bytes_accessed=4 * (2 * own.size + 2 * south.size + chosen.size),
            transcendentals=0,
        ),
    )(substeps, own, south, north, chosen, south_courant, north_courant, emissions)


def shards(tracers, emissions, winds, diffusivity, substeps, loader):
    tiles = lax.axis_size("tile")
    tile_position = lax.axis_index("tile")
    tile_numbers = jnp.arange(substeps.shape[0])
    loader_slot = jnp.sum(jnp.where(tile_numbers == tile_position, loader, 0))
    levels = tracers.shape[1]
    height = tracers.shape[2]
    width = tracers.shape[3]
    halo = ROUNDS

    local = jnp.concatenate(
        [winds[0].reshape(2 * levels, height, width), diffusivity[0]], axis=0
    )
    by_row = jnp.transpose(tracers, (2, 1, 0, 3))
    chosen, south_rows, north_rows, south_courant, north_courant = exchange(
        local, by_row, loader_slot, halo, 2 * levels
    )
    mixed = transport(
        substeps, by_row, south_rows, north_rows, chosen, south_courant,
        north_courant, jnp.transpose(emissions, (1, 0, 2)),
    )
    return jnp.transpose(mixed, (2, 1, 0, 3))


def solution(mesh):
    return jax.shard_map(
        shards,
        mesh=mesh,
        in_specs=(
            P("group", None, "tile", None),
            P("group", "tile", None),
            P("group", None, None, "tile", None),
            P("group", None, "tile", None),
            P(),
            P(),
        ),
        out_specs=P("group", None, "tile", None),
        check_vma=False,
    )
```

```python
import jax
import jax.numpy as jnp
from jax import lax
from jax.experimental import pallas as pl
from jax.experimental.pallas import tpu as pltpu
from jax.sharding import PartitionSpec as P

ROUNDS = 6


def from_behind(value, axis, by):
    count = lax.axis_size(axis)
    pairs = [(i, i + by) for i in range(count) if 0 <= i + by < count]
    return lax.ppermute(value, axis, pairs)


def exchange_kernel(
    masked, up, down, chosen, south, north, south_courant, north_courant,
    total, received, send_sems, recv_sems,
):
    mesh = pl.DeviceIdType.MESH
    tiles = lax.axis_size("tile")
    bits = lax.axis_size("group").bit_length() - 1
    tile = lax.axis_index("tile")
    me = lax.axis_index("group")
    core = me % 2
    half = masked.shape[0] // 2
    planes = south_courant.shape[0]

    def partner(bit):
        return me + (1 << bit) * (1 - 2 * ((me // (1 << bit)) % 2))

    barrier = pltpu.get_barrier_semaphore()
    for bit in range(bits):
        pl.semaphore_signal(barrier, 1, device_id=(tile, partner(bit)), device_id_type=mesh)

    @pl.when(tile > 0)
    def _():
        pl.semaphore_signal(barrier, 1, device_id=(tile - 1, me), device_id_type=mesh)

    @pl.when(tile < tiles - 1)
    def _():
        pl.semaphore_signal(barrier, 1, device_id=(tile + 1, me), device_id_type=mesh)

    has_south = (tile + tiles - 1) // tiles
    has_north = (2 * tiles - 3 - tile) // (tiles - 1)
    pl.semaphore_wait(barrier, bits + has_south + has_north)

    def along_tile(source, target, slot, by):
        return pltpu.make_async_remote_copy(
            src_ref=source, dst_ref=target, send_sem=send_sems.at[slot],
            recv_sem=recv_sems.at[slot], device_id=(tile + by, me), device_id_type=mesh,
        )

    @pl.when(tile == 0)
    def _():
        south[...] = jnp.zeros_like(south)
        south_courant[...] = jnp.zeros_like(south_courant)

    @pl.when(tile == tiles - 1)
    def _():
        north[...] = jnp.zeros_like(north)
        north_courant[...] = jnp.zeros_like(north_courant)

    def along_group(source, bit, slot):
        copy = pltpu.make_async_remote_copy(
            src_ref=source, dst_ref=received.at[slot], send_sem=send_sems.at[2 + slot],
            recv_sem=recv_sems.at[2 + slot], device_id=(tile, partner(bit)),
            device_id_type=mesh,
        )
        copy.start()
        copy.wait()

    along_group(masked.at[pl.ds((1 - core) * half, half)], 0, 0)
    total[...] = masked[pl.ds(core * half, half)] + received[0]
    for bit in range(1, bits):
        along_group(total, bit, bit)
        total[...] = total[...] + received[bit]
        if bit == 2:
            @pl.when(tile < tiles - 1)
            def _():
                along_tile(up, south, 0, 1).start()

            @pl.when(tile > 0)
            def _():
                along_tile(down, north, 1, -1).start()
    along_group(total, 0, bits)
    chosen[pl.ds(core * half, half)] = total[...]
    chosen[pl.ds((1 - core) * half, half)] = received[bits]

    @pl.when(tile < tiles - 1)
    def _():
        along_tile(chosen.at[pl.ds(0, planes)], south_courant, 2 + bits + 1, 1).start()

    @pl.when(tile > 0)
    def _():
        along_tile(chosen.at[pl.ds(0, planes)], north_courant, 2 + bits + 2, -1).start()

    @pl.when(tile < tiles - 1)
    def _():
        along_tile(up, south, 0, 1).wait_send()
        along_tile(chosen.at[pl.ds(0, planes)], south_courant, 2 + bits + 1, 1).wait_send()
        along_tile(up, north, 1, 1).wait_recv()
        along_tile(chosen.at[pl.ds(0, planes)], north_courant, 2 + bits + 2, 1).wait_recv()

    @pl.when(tile > 0)
    def _():
        along_tile(down, north, 1, -1).wait_send()
        along_tile(chosen.at[pl.ds(0, planes)], north_courant, 2 + bits + 2, -1).wait_send()
        along_tile(down, south, 0, -1).wait_recv()
        along_tile(chosen.at[pl.ds(0, planes)], south_courant, 2 + bits + 1, -1).wait_recv()


def exchange(value, by_row, root, halo, planes):
    groups = lax.axis_size("group")
    assert groups & (groups - 1) == 0 and groups >= 2
    bits = groups.bit_length() - 1
    half = -(-value.shape[0] // 2)
    padded = jnp.concatenate(
        [value, jnp.zeros((2 * half - value.shape[0],) + value.shape[1:], value.dtype)]
    )
    masked = jnp.where(lax.axis_index("group") == root, padded, jnp.zeros_like(padded))
    height = by_row.shape[0]
    vmem = pl.BlockSpec(memory_space=pltpu.VMEM)
    rows = jax.ShapeDtypeStruct((halo,) + by_row.shape[1:], by_row.dtype)
    winds = jax.ShapeDtypeStruct((planes,) + value.shape[1:], value.dtype)
    return pl.pallas_call(
        exchange_kernel,
        out_shape=(jax.ShapeDtypeStruct(padded.shape, padded.dtype), rows, rows, winds, winds),
        in_specs=[vmem] * 3,
        out_specs=(vmem,) * 5,
        scratch_shapes=[
            pltpu.VMEM((half,) + value.shape[1:], value.dtype),
            pltpu.VMEM((bits + 1, half) + value.shape[1:], value.dtype),
            pltpu.SemaphoreType.DMA((bits + 5,)),
            pltpu.SemaphoreType.DMA((bits + 5,)),
        ],
        compiler_params=pltpu.CompilerParams(collective_id=0, has_side_effects=True),
    )(masked, by_row[height - halo :], by_row[:halo])


def transport_kernel(
    substeps, own, south, north, chosen, south_courant, north_courant, emissions, out,
    held, pivots, ratios, lowers, planes, fractions,
):
    levels, height, tracer_count, width = held.shape
    halo = south.shape[0]
    rows = height + 2 * halo
    lane_shape = (tracer_count, width)

    def spread(row_ref, row):
        return jnp.broadcast_to(row_ref[pl.ds(row, 1), :], lane_shape)

    tiles = substeps.shape[0]
    tile_position = lax.axis_index("tile")
    courant = chosen
    coefficient = chosen.at[pl.ds(2 * levels, levels - 1)]

    def _prepare():
        bands = (
            jnp.maximum(tile_position - 1, 0),
            tile_position,
            jnp.minimum(tile_position + 1, tiles - 1),
        )
        for band, position in enumerate(bands):
            count = substeps[position]
            spread_count = jnp.full(lane_shape, count.astype(jnp.float32))
            for substep in range(ROUNDS):
                fractions[3 * substep + band] = jnp.where(
                    substep < count, 1.0 / spread_count, jnp.float32(0.0)
                )
        zero_plane = jnp.zeros((height, width), jnp.float32)
        previous_ratio = zero_plane
        for lev in range(levels):
            lower_coef = coefficient[lev - 1] if lev > 0 else zero_plane
            upper_coef = coefficient[lev] if lev < levels - 1 else zero_plane
            pivot = 1.0 / (1.0 + lower_coef + upper_coef - lower_coef * previous_ratio)
            previous_ratio = upper_coef * pivot
            planes[0] = pivot
            planes[1] = previous_ratio
            planes[2] = lower_coef
            for row in range(height):
                pivots[lev, row] = spread(planes.at[0], row)
                ratios[lev, row] = spread(planes.at[1], row)
                lowers[lev, row] = spread(planes.at[2], row)

    _prepare()

    def advect(level, carry):
        def wind_row(component, row):
            index = component * levels + level
            if row < halo:
                return spread(south_courant.at[index], row + height - halo)
            if row < halo + height:
                return spread(courant.at[index], row - halo)
            return spread(north_courant.at[index], row - halo - height)

        first_row = jnp.where(tile_position > 0, jnp.float32(1.0), jnp.float32(0.0))
        zonal_up, zonal_down, merid_up, merid_down = [], [], [], []
        for row in range(rows):
            zonal = wind_row(0, row)
            meridional = wind_row(1, row)
            if row == halo:
                meridional = meridional * first_row
            zonal_up.append(jnp.maximum(zonal, 0.0))
            zonal_down.append(jnp.minimum(zonal, 0.0))
            merid_up.append(jnp.maximum(meridional, 0.0))
            merid_down.append(jnp.minimum(meridional, 0.0))

        mixing = [south[row, level] for row in range(halo)]
        mixing += [own[row, level] for row in range(height)]
        mixing += [north[row, level] for row in range(halo)]
        for substep in range(ROUNDS):
            low, high = substep + 1, rows - 2 - substep
            south_flux = {}
            for row in range(low, high + 2):
                south_flux[row] = merid_up[row] * mixing[row - 1] + merid_down[row] * mixing[row]
            advanced = list(mixing)
            for row in range(low, high + 1):
                band = 0 if row < halo else (1 if row < halo + height else 2)
                fraction = fractions[3 * substep + band]
                from_west = pltpu.roll(mixing[row], 1, 1)
                west_flux = zonal_up[row] * from_west + zonal_down[row] * mixing[row]
                east_flux = pltpu.roll(west_flux, width - 1, 1)
                advanced[row] = mixing[row] - fraction * (
                    (east_flux - west_flux) + (south_flux[row + 1] - south_flux[row])
                )
            mixing = advanced
        for row in range(height):
            held[level, row] = mixing[halo + row]
        return carry

    lax.fori_loop(0, levels, advect, 0)

    def _finish():
        for row in range(height):
            held[0, row] = held[0, row] + emissions[row]
            previous_value = jnp.zeros(lane_shape, jnp.float32)
            for lev in range(levels):
                previous_value = (
                    held[lev, row] + lowers[lev, row] * previous_value
                ) * pivots[lev, row]
                held[lev, row] = previous_value
            current = held[levels - 1, row]
            out[row, levels - 1] = current
            for lev in range(levels - 2, -1, -1):
                current = held[lev, row] + ratios[lev, row] * current
                out[row, lev] = current

    _finish()


def transport(substeps, own, south, north, chosen, south_courant, north_courant,
              emissions):
    height, levels, tracer_count, width = own.shape
    vmem = pl.BlockSpec(memory_space=pltpu.VMEM)
    table = pltpu.VMEM((levels, height, tracer_count, width), jnp.float32)
    return pl.pallas_call(
        transport_kernel,
        out_shape=jax.ShapeDtypeStruct(own.shape, jnp.float32),
        in_specs=[pl.BlockSpec(memory_space=pltpu.SMEM)] + [vmem] * 7,
        out_specs=vmem,
        scratch_shapes=[
            table,
            table,
            table,
            table,
            pltpu.VMEM((3, height, width), jnp.float32),
            pltpu.VMEM((3 * ROUNDS, tracer_count, width), jnp.float32),
        ],
        cost_estimate=pl.CostEstimate(
            flops=levels * tracer_count * width * 78 * 14,
            bytes_accessed=4 * (2 * own.size + 2 * south.size + chosen.size),
            transcendentals=0,
        ),
    )(substeps, own, south, north, chosen, south_courant, north_courant, emissions)


def shards(tracers, emissions, winds, diffusivity, substeps, loader):
    tiles = lax.axis_size("tile")
    tile_position = lax.axis_index("tile")
    tile_numbers = jnp.arange(substeps.shape[0])
    loader_slot = jnp.sum(jnp.where(tile_numbers == tile_position, loader, 0))
    levels = tracers.shape[1]
    height = tracers.shape[2]
    width = tracers.shape[3]
    halo = ROUNDS

    local = jnp.concatenate(
        [winds[0].reshape(2 * levels, height, width), diffusivity[0]], axis=0
    )
    by_row = jnp.transpose(tracers, (2, 1, 0, 3))
    chosen, south_rows, north_rows, south_courant, north_courant = exchange(
        local, by_row, loader_slot, halo, 2 * levels
    )
    mixed = transport(
        substeps, by_row, south_rows, north_rows, chosen, south_courant,
        north_courant, jnp.transpose(emissions, (1, 0, 2)),
    )
    return jnp.transpose(mixed, (2, 1, 0, 3))


def solution(mesh):
    return jax.shard_map(
        shards,
        mesh=mesh,
        in_specs=(
            P("group", None, "tile", None),
            P("group", "tile", None),
            P("group", None, None, "tile", None),
            P("group", None, "tile", None),
            P(),
            P(),
        ),
        out_specs=P("group", None, "tile", None),
        check_vma=False,
    )
```

```python
import jax
import jax.numpy as jnp
from jax import lax
from jax.experimental import pallas as pl
from jax.experimental.pallas import tpu as pltpu
from jax.sharding import PartitionSpec as P

ROUNDS = 6


def from_behind(value, axis, by):
    count = lax.axis_size(axis)
    pairs = [(i, i + by) for i in range(count) if 0 <= i + by < count]
    return lax.ppermute(value, axis, pairs)


def exchange_kernel(
    masked, up, down, chosen, south, north, south_courant, north_courant,
    total, received, send_sems, recv_sems,
):
    mesh = pl.DeviceIdType.MESH
    tiles = lax.axis_size("tile")
    bits = lax.axis_size("group").bit_length() - 1
    tile = lax.axis_index("tile")
    me = lax.axis_index("group")
    core = me % 2
    half = masked.shape[0] // 2
    planes = south_courant.shape[0]

    def partner(bit):
        return me + (1 << bit) * (1 - 2 * ((me // (1 << bit)) % 2))

    barrier = pltpu.get_barrier_semaphore()
    for bit in range(bits):
        pl.semaphore_signal(barrier, 1, device_id=(tile, partner(bit)), device_id_type=mesh)

    @pl.when(tile > 0)
    def _():
        pl.semaphore_signal(barrier, 1, device_id=(tile - 1, me), device_id_type=mesh)

    @pl.when(tile < tiles - 1)
    def _():
        pl.semaphore_signal(barrier, 1, device_id=(tile + 1, me), device_id_type=mesh)

    has_south = (tile + tiles - 1) // tiles
    has_north = (2 * tiles - 3 - tile) // (tiles - 1)
    pl.semaphore_wait(barrier, bits + has_south + has_north)

    def along_tile(source, target, slot, by):
        return pltpu.make_async_remote_copy(
            src_ref=source, dst_ref=target, send_sem=send_sems.at[slot],
            recv_sem=recv_sems.at[slot], device_id=(tile + by, me), device_id_type=mesh,
        )

    @pl.when(tile == 0)
    def _():
        south[...] = jnp.zeros_like(south)
        south_courant[...] = jnp.zeros_like(south_courant)

    @pl.when(tile == tiles - 1)
    def _():
        north[...] = jnp.zeros_like(north)
        north_courant[...] = jnp.zeros_like(north_courant)

    def along_group(source, bit, slot):
        copy = pltpu.make_async_remote_copy(
            src_ref=source, dst_ref=received.at[slot], send_sem=send_sems.at[2 + slot],
            recv_sem=recv_sems.at[2 + slot], device_id=(tile, partner(bit)),
            device_id_type=mesh,
        )
        copy.start()
        copy.wait()

    along_group(masked.at[pl.ds((1 - core) * half, half)], 0, 0)
    total[...] = masked[pl.ds(core * half, half)] + received[0]
    for bit in range(1, bits):
        along_group(total, bit, bit)
        total[...] = total[...] + received[bit]
        if bit == 1:
            @pl.when(tile < tiles - 1)
            def _():
                along_tile(up, south, 0, 1).start()

            @pl.when(tile > 0)
            def _():
                along_tile(down, north, 1, -1).start()
    along_group(total, 0, bits)
    chosen[pl.ds(core * half, half)] = total[...]
    chosen[pl.ds((1 - core) * half, half)] = received[bits]

    @pl.when(tile < tiles - 1)
    def _():
        along_tile(chosen.at[pl.ds(0, planes)], south_courant, 2 + bits + 1, 1).start()

    @pl.when(tile > 0)
    def _():
        along_tile(chosen.at[pl.ds(0, planes)], north_courant, 2 + bits + 2, -1).start()

    @pl.when(tile < tiles - 1)
    def _():
        along_tile(up, south, 0, 1).wait_send()
        along_tile(chosen.at[pl.ds(0, planes)], south_courant, 2 + bits + 1, 1).wait_send()
        along_tile(up, north, 1, 1).wait_recv()
        along_tile(chosen.at[pl.ds(0, planes)], north_courant, 2 + bits + 2, 1).wait_recv()

    @pl.when(tile > 0)
    def _():
        along_tile(down, north, 1, -1).wait_send()
        along_tile(chosen.at[pl.ds(0, planes)], north_courant, 2 + bits + 2, -1).wait_send()
        along_tile(down, south, 0, -1).wait_recv()
        along_tile(chosen.at[pl.ds(0, planes)], south_courant, 2 + bits + 1, -1).wait_recv()


def exchange(value, by_row, root, halo, planes):
    groups = lax.axis_size("group")
    assert groups & (groups - 1) == 0 and groups >= 2
    bits = groups.bit_length() - 1
    half = -(-value.shape[0] // 2)
    padded = jnp.concatenate(
        [value, jnp.zeros((2 * half - value.shape[0],) + value.shape[1:], value.dtype)]
    )
    masked = jnp.where(lax.axis_index("group") == root, padded, jnp.zeros_like(padded))
    height = by_row.shape[0]
    vmem = pl.BlockSpec(memory_space=pltpu.VMEM)
    rows = jax.ShapeDtypeStruct((halo,) + by_row.shape[1:], by_row.dtype)
    winds = jax.ShapeDtypeStruct((planes,) + value.shape[1:], value.dtype)
    return pl.pallas_call(
        exchange_kernel,
        out_shape=(jax.ShapeDtypeStruct(padded.shape, padded.dtype), rows, rows, winds, winds),
        in_specs=[vmem] * 3,
        out_specs=(vmem,) * 5,
        scratch_shapes=[
            pltpu.VMEM((half,) + value.shape[1:], value.dtype),
            pltpu.VMEM((bits + 1, half) + value.shape[1:], value.dtype),
            pltpu.SemaphoreType.DMA((bits + 5,)),
            pltpu.SemaphoreType.DMA((bits + 5,)),
        ],
        compiler_params=pltpu.CompilerParams(collective_id=0, has_side_effects=True),
    )(masked, by_row[height - halo :], by_row[:halo])


def transport_kernel(
    substeps, own, south, north, chosen, south_courant, north_courant, emissions, out,
    held, pivots, ratios, lowers, planes, fractions, winds,
):
    levels, height, tracer_count, width = held.shape
    halo = south.shape[0]
    rows = height + 2 * halo
    lane_shape = (tracer_count, width)

    def spread(row_ref, row):
        return jnp.broadcast_to(row_ref[pl.ds(row, 1), :], lane_shape)

    tiles = substeps.shape[0]
    tile_position = lax.axis_index("tile")
    courant = chosen
    coefficient = chosen.at[pl.ds(2 * levels, levels - 1)]

    def _prepare():
        bands = (
            jnp.maximum(tile_position - 1, 0),
            tile_position,
            jnp.minimum(tile_position + 1, tiles - 1),
        )
        for band, position in enumerate(bands):
            count = substeps[position]
            spread_count = jnp.full(lane_shape, count.astype(jnp.float32))
            for substep in range(ROUNDS):
                fractions[3 * substep + band] = jnp.where(
                    substep < count, 1.0 / spread_count, jnp.float32(0.0)
                )
        zero_plane = jnp.zeros((height, width), jnp.float32)
        previous_ratio = zero_plane
        for lev in range(levels):
            lower_coef = coefficient[lev - 1] if lev > 0 else zero_plane
            upper_coef = coefficient[lev] if lev < levels - 1 else zero_plane
            pivot = 1.0 / (1.0 + lower_coef + upper_coef - lower_coef * previous_ratio)
            previous_ratio = upper_coef * pivot
            planes[0] = pivot
            planes[1] = previous_ratio
            planes[2] = lower_coef
            for row in range(height):
                pivots[lev, row] = spread(planes.at[0], row)
                ratios[lev, row] = spread(planes.at[1], row)
                lowers[lev, row] = spread(planes.at[2], row)

    _prepare()

    def prepare_winds(level, carry):
        def wind_row(component, row):
            index = component * levels + level
            if row < halo:
                return spread(south_courant.at[index], row + height - halo)
            if row < halo + height:
                return spread(courant.at[index], row - halo)
            return spread(north_courant.at[index], row - halo - height)

        first_row = jnp.where(tile_position > 0, jnp.float32(1.0), jnp.float32(0.0))
        for row in range(rows):
            zonal = wind_row(0, row)
            meridional = wind_row(1, row)
            if row == halo:
                meridional = meridional * first_row
            winds[level, row, 0] = jnp.maximum(zonal, 0.0)
            winds[level, row, 1] = jnp.minimum(zonal, 0.0)
            winds[level, row, 2] = jnp.maximum(meridional, 0.0)
            winds[level, row, 3] = jnp.minimum(meridional, 0.0)
        return carry

    lax.fori_loop(0, levels, prepare_winds, 0)

    def advect(level, carry):
        def wind(row, part):
            return winds[level, row, part]

        mixing = [south[row, level] for row in range(halo)]
        mixing += [own[row, level] for row in range(height)]
        mixing += [north[row, level] for row in range(halo)]
        for substep in range(ROUNDS):
            low, high = substep + 1, rows - 2 - substep
            south_flux = {}
            for row in range(low, high + 2):
                south_flux[row] = wind(row, 2) * mixing[row - 1] + wind(row, 3) * mixing[row]
            advanced = list(mixing)
            for row in range(low, high + 1):
                band = 0 if row < halo else (1 if row < halo + height else 2)
                fraction = fractions[3 * substep + band]
                from_west = pltpu.roll(mixing[row], 1, 1)
                west_flux = wind(row, 0) * from_west + wind(row, 1) * mixing[row]
                east_flux = pltpu.roll(west_flux, width - 1, 1)
                advanced[row] = mixing[row] - fraction * (
                    (east_flux - west_flux) + (south_flux[row + 1] - south_flux[row])
                )
            mixing = advanced
        for row in range(height):
            held[level, row] = mixing[halo + row]
        return carry

    lax.fori_loop(0, levels, advect, 0)

    def _finish():
        for row in range(height):
            held[0, row] = held[0, row] + emissions[row]
            previous_value = jnp.zeros(lane_shape, jnp.float32)
            for lev in range(levels):
                previous_value = (
                    held[lev, row] + lowers[lev, row] * previous_value
                ) * pivots[lev, row]
                held[lev, row] = previous_value
            current = held[levels - 1, row]
            out[row, levels - 1] = current
            for lev in range(levels - 2, -1, -1):
                current = held[lev, row] + ratios[lev, row] * current
                out[row, lev] = current

    _finish()


def transport(substeps, own, south, north, chosen, south_courant, north_courant,
              emissions):
    height, levels, tracer_count, width = own.shape
    vmem = pl.BlockSpec(memory_space=pltpu.VMEM)
    table = pltpu.VMEM((levels, height, tracer_count, width), jnp.float32)
    return pl.pallas_call(
        transport_kernel,
        out_shape=jax.ShapeDtypeStruct(own.shape, jnp.float32),
        in_specs=[pl.BlockSpec(memory_space=pltpu.SMEM)] + [vmem] * 7,
        out_specs=vmem,
        scratch_shapes=[
            table,
            table,
            table,
            table,
            pltpu.VMEM((3, height, width), jnp.float32),
            pltpu.VMEM((3 * ROUNDS, tracer_count, width), jnp.float32),
            pltpu.VMEM((levels, height + 2 * south.shape[0], 4, tracer_count, width), jnp.float32),
        ],
        cost_estimate=pl.CostEstimate(
            flops=levels * tracer_count * width * 78 * 14,
            bytes_accessed=4 * (2 * own.size + 2 * south.size + chosen.size),
            transcendentals=0,
        ),
    )(substeps, own, south, north, chosen, south_courant, north_courant, emissions)


def shards(tracers, emissions, winds, diffusivity, substeps, loader):
    tiles = lax.axis_size("tile")
    tile_position = lax.axis_index("tile")
    tile_numbers = jnp.arange(substeps.shape[0])
    loader_slot = jnp.sum(jnp.where(tile_numbers == tile_position, loader, 0))
    levels = tracers.shape[1]
    height = tracers.shape[2]
    width = tracers.shape[3]
    halo = ROUNDS

    local = jnp.concatenate(
        [winds[0].reshape(2 * levels, height, width), diffusivity[0]], axis=0
    )
    by_row = jnp.transpose(tracers, (2, 1, 0, 3))
    chosen, south_rows, north_rows, south_courant, north_courant = exchange(
        local, by_row, loader_slot, halo, 2 * levels
    )
    mixed = transport(
        substeps, by_row, south_rows, north_rows, chosen, south_courant,
        north_courant, jnp.transpose(emissions, (1, 0, 2)),
    )
    return jnp.transpose(mixed, (2, 1, 0, 3))


def solution(mesh):
    return jax.shard_map(
        shards,
        mesh=mesh,
        in_specs=(
            P("group", None, "tile", None),
            P("group", "tile", None),
            P("group", None, None, "tile", None),
            P("group", None, "tile", None),
            P(),
            P(),
        ),
        out_specs=P("group", None, "tile", None),
        check_vma=False,
    )
```

```python
import jax
import jax.numpy as jnp
from jax import lax
from jax.experimental import pallas as pl
from jax.experimental.pallas import tpu as pltpu
from jax.sharding import PartitionSpec as P

ROUNDS = 6


def from_behind(value, axis, by):
    count = lax.axis_size(axis)
    pairs = [(i, i + by) for i in range(count) if 0 <= i + by < count]
    return lax.ppermute(value, axis, pairs)


def exchange_kernel(
    masked, up, down, chosen, south, north, south_courant, north_courant,
    total, received, send_sems, recv_sems,
):
    mesh = pl.DeviceIdType.MESH
    tiles = lax.axis_size("tile")
    bits = lax.axis_size("group").bit_length() - 1
    tile = lax.axis_index("tile")
    me = lax.axis_index("group")
    core = me % 2
    half = masked.shape[0] // 2
    planes = south_courant.shape[0]
    halo = south_courant.shape[1]
    rows_from = chosen.shape[1] - halo

    def partner(bit):
        return me + (1 << bit) * (1 - 2 * ((me // (1 << bit)) % 2))

    barrier = pltpu.get_barrier_semaphore()
    for bit in range(bits):
        pl.semaphore_signal(barrier, 1, device_id=(tile, partner(bit)), device_id_type=mesh)

    @pl.when(tile > 0)
    def _():
        pl.semaphore_signal(barrier, 1, device_id=(tile - 1, me), device_id_type=mesh)

    @pl.when(tile < tiles - 1)
    def _():
        pl.semaphore_signal(barrier, 1, device_id=(tile + 1, me), device_id_type=mesh)

    has_south = (tile + tiles - 1) // tiles
    has_north = (2 * tiles - 3 - tile) // (tiles - 1)
    pl.semaphore_wait(barrier, bits + has_south + has_north)

    def along_tile(source, target, slot, by):
        return pltpu.make_async_remote_copy(
            src_ref=source, dst_ref=target, send_sem=send_sems.at[slot],
            recv_sem=recv_sems.at[slot], device_id=(tile + by, me), device_id_type=mesh,
        )

    @pl.when(tile == 0)
    def _():
        south[...] = jnp.zeros_like(south)
        south_courant[...] = jnp.zeros_like(south_courant)

    @pl.when(tile == tiles - 1)
    def _():
        north[...] = jnp.zeros_like(north)
        north_courant[...] = jnp.zeros_like(north_courant)

    def along_group(source, bit, slot):
        copy = pltpu.make_async_remote_copy(
            src_ref=source, dst_ref=received.at[slot], send_sem=send_sems.at[2 + slot],
            recv_sem=recv_sems.at[2 + slot], device_id=(tile, partner(bit)),
            device_id_type=mesh,
        )
        copy.start()
        copy.wait()

    along_group(masked.at[pl.ds((1 - core) * half, half)], 0, 0)
    total[...] = masked[pl.ds(core * half, half)] + received[0]
    for bit in range(1, bits):
        along_group(total, bit, bit)
        total[...] = total[...] + received[bit]
        if bit == 1:
            @pl.when(tile < tiles - 1)
            def _():
                along_tile(up, south, 0, 1).start()

            @pl.when(tile > 0)
            def _():
                along_tile(down, north, 1, -1).start()
    along_group(total, 0, bits)
    chosen[pl.ds(core * half, half)] = total[...]
    chosen[pl.ds((1 - core) * half, half)] = received[bits]

    @pl.when(tile < tiles - 1)
    def _():
        along_tile(chosen.at[pl.ds(0, planes), pl.ds(rows_from, halo)], south_courant, 2 + bits + 1, 1).start()

    @pl.when(tile > 0)
    def _():
        along_tile(chosen.at[pl.ds(0, planes), pl.ds(0, halo)], north_courant, 2 + bits + 2, -1).start()

    @pl.when(tile < tiles - 1)
    def _():
        along_tile(up, south, 0, 1).wait_send()
        along_tile(chosen.at[pl.ds(0, planes), pl.ds(rows_from, halo)], south_courant, 2 + bits + 1, 1).wait_send()
        along_tile(up, north, 1, 1).wait_recv()
        along_tile(chosen.at[pl.ds(0, planes), pl.ds(0, halo)], north_courant, 2 + bits + 2, 1).wait_recv()

    @pl.when(tile > 0)
    def _():
        along_tile(down, north, 1, -1).wait_send()
        along_tile(chosen.at[pl.ds(0, planes), pl.ds(0, halo)], north_courant, 2 + bits + 2, -1).wait_send()
        along_tile(down, south, 0, -1).wait_recv()
        along_tile(chosen.at[pl.ds(0, planes), pl.ds(rows_from, halo)], south_courant, 2 + bits + 1, -1).wait_recv()


def exchange(value, by_row, root, halo, planes):
    groups = lax.axis_size("group")
    assert groups & (groups - 1) == 0 and groups >= 2
    bits = groups.bit_length() - 1
    half = -(-value.shape[0] // 2)
    padded = jnp.concatenate(
        [value, jnp.zeros((2 * half - value.shape[0],) + value.shape[1:], value.dtype)]
    )
    masked = jnp.where(lax.axis_index("group") == root, padded, jnp.zeros_like(padded))
    height = by_row.shape[0]
    vmem = pl.BlockSpec(memory_space=pltpu.VMEM)
    rows = jax.ShapeDtypeStruct((halo,) + by_row.shape[1:], by_row.dtype)
    winds = jax.ShapeDtypeStruct((planes, halo) + value.shape[2:], value.dtype)
    return pl.pallas_call(
        exchange_kernel,
        out_shape=(jax.ShapeDtypeStruct(padded.shape, padded.dtype), rows, rows, winds, winds),
        in_specs=[vmem] * 3,
        out_specs=(vmem,) * 5,
        scratch_shapes=[
            pltpu.VMEM((half,) + value.shape[1:], value.dtype),
            pltpu.VMEM((bits + 1, half) + value.shape[1:], value.dtype),
            pltpu.SemaphoreType.DMA((bits + 5,)),
            pltpu.SemaphoreType.DMA((bits + 5,)),
        ],
        compiler_params=pltpu.CompilerParams(collective_id=0, has_side_effects=True),
    )(masked, by_row[height - halo :], by_row[:halo])


def transport_kernel(
    substeps, own, south, north, chosen, south_courant, north_courant, emissions, out,
    held, pivots, ratios, lowers, planes, fractions,
):
    levels, height, tracer_count, width = held.shape
    halo = south.shape[0]
    rows = height + 2 * halo
    lane_shape = (tracer_count, width)

    def spread(row_ref, row):
        return jnp.broadcast_to(row_ref[pl.ds(row, 1), :], lane_shape)

    tiles = substeps.shape[0]
    tile_position = lax.axis_index("tile")
    courant = chosen
    coefficient = chosen.at[pl.ds(2 * levels, levels - 1)]

    def _prepare():
        bands = (
            jnp.maximum(tile_position - 1, 0),
            tile_position,
            jnp.minimum(tile_position + 1, tiles - 1),
        )
        for band, position in enumerate(bands):
            count = substeps[position]
            spread_count = jnp.full(lane_shape, count.astype(jnp.float32))
            for substep in range(ROUNDS):
                fractions[3 * substep + band] = jnp.where(
                    substep < count, 1.0 / spread_count, jnp.float32(0.0)
                )
        zero_plane = jnp.zeros((height, width), jnp.float32)
        previous_ratio = zero_plane
        for lev in range(levels):
            lower_coef = coefficient[lev - 1] if lev > 0 else zero_plane
            upper_coef = coefficient[lev] if lev < levels - 1 else zero_plane
            pivot = 1.0 / (1.0 + lower_coef + upper_coef - lower_coef * previous_ratio)
            previous_ratio = upper_coef * pivot
            planes[0] = pivot
            planes[1] = previous_ratio
            planes[2] = lower_coef
            for row in range(height):
                pivots[lev, row] = spread(planes.at[0], row)
                ratios[lev, row] = spread(planes.at[1], row)
                lowers[lev, row] = spread(planes.at[2], row)

    _prepare()

    def advect(level, carry):
        def wind_row(component, row):
            index = component * levels + level
            if row < halo:
                return spread(south_courant.at[index], row)
            if row < halo + height:
                return spread(courant.at[index], row - halo)
            return spread(north_courant.at[index], row - halo - height)

        first_row = jnp.where(tile_position > 0, jnp.float32(1.0), jnp.float32(0.0))
        zonal_up, zonal_down, merid_up, merid_down = [], [], [], []
        for row in range(rows):
            zonal = wind_row(0, row)
            meridional = wind_row(1, row)
            if row == halo:
                meridional = meridional * first_row
            zonal_up.append(jnp.maximum(zonal, 0.0))
            zonal_down.append(jnp.minimum(zonal, 0.0))
            merid_up.append(jnp.maximum(meridional, 0.0))
            merid_down.append(jnp.minimum(meridional, 0.0))

        mixing = [south[row, level] for row in range(halo)]
        mixing += [own[row, level] for row in range(height)]
        mixing += [north[row, level] for row in range(halo)]
        for substep in range(ROUNDS):
            low, high = substep + 1, rows - 2 - substep
            south_flux = {}
            for row in range(low, high + 2):
                south_flux[row] = merid_up[row] * mixing[row - 1] + merid_down[row] * mixing[row]
            advanced = list(mixing)
            for row in range(low, high + 1):
                band = 0 if row < halo else (1 if row < halo + height else 2)
                fraction = fractions[3 * substep + band]
                from_west = pltpu.roll(mixing[row], 1, 1)
                west_flux = zonal_up[row] * from_west + zonal_down[row] * mixing[row]
                east_flux = pltpu.roll(west_flux, width - 1, 1)
                advanced[row] = mixing[row] - fraction * (
                    (east_flux - west_flux) + (south_flux[row + 1] - south_flux[row])
                )
            mixing = advanced
        for row in range(height):
            held[level, row] = mixing[halo + row]
        return carry

    lax.fori_loop(0, levels, advect, 0)

    def _finish():
        for row in range(height):
            held[0, row] = held[0, row] + emissions[row]
            previous_value = jnp.zeros(lane_shape, jnp.float32)
            for lev in range(levels):
                previous_value = (
                    held[lev, row] + lowers[lev, row] * previous_value
                ) * pivots[lev, row]
                held[lev, row] = previous_value
            current = held[levels - 1, row]
            out[row, levels - 1] = current
            for lev in range(levels - 2, -1, -1):
                current = held[lev, row] + ratios[lev, row] * current
                out[row, lev] = current

    _finish()


def transport(substeps, own, south, north, chosen, south_courant, north_courant,
              emissions):
    height, levels, tracer_count, width = own.shape
    vmem = pl.BlockSpec(memory_space=pltpu.VMEM)
    table = pltpu.VMEM((levels, height, tracer_count, width), jnp.float32)
    return pl.pallas_call(
        transport_kernel,
        out_shape=jax.ShapeDtypeStruct(own.shape, jnp.float32),
        in_specs=[pl.BlockSpec(memory_space=pltpu.SMEM)] + [vmem] * 7,
        out_specs=vmem,
        scratch_shapes=[
            table,
            table,
            table,
            table,
            pltpu.VMEM((3, height, width), jnp.float32),
            pltpu.VMEM((3 * ROUNDS, tracer_count, width), jnp.float32),
        ],
        cost_estimate=pl.CostEstimate(
            flops=levels * tracer_count * width * 78 * 14,
            bytes_accessed=4 * (2 * own.size + 2 * south.size + chosen.size),
            transcendentals=0,
        ),
    )(substeps, own, south, north, chosen, south_courant, north_courant, emissions)


def shards(tracers, emissions, winds, diffusivity, substeps, loader):
    tiles = lax.axis_size("tile")
    tile_position = lax.axis_index("tile")
    tile_numbers = jnp.arange(substeps.shape[0])
    loader_slot = jnp.sum(jnp.where(tile_numbers == tile_position, loader, 0))
    levels = tracers.shape[1]
    height = tracers.shape[2]
    width = tracers.shape[3]
    halo = ROUNDS

    local = jnp.concatenate(
        [winds[0].reshape(2 * levels, height, width), diffusivity[0]], axis=0
    )
    by_row = jnp.transpose(tracers, (2, 1, 0, 3))
    chosen, south_rows, north_rows, south_courant, north_courant = exchange(
        local, by_row, loader_slot, halo, 2 * levels
    )
    mixed = transport(
        substeps, by_row, south_rows, north_rows, chosen, south_courant,
        north_courant, jnp.transpose(emissions, (1, 0, 2)),
    )
    return jnp.transpose(mixed, (2, 1, 0, 3))


def solution(mesh):
    return jax.shard_map(
        shards,
        mesh=mesh,
        in_specs=(
            P("group", None, "tile", None),
            P("group", "tile", None),
            P("group", None, None, "tile", None),
            P("group", None, "tile", None),
            P(),
            P(),
        ),
        out_specs=P("group", None, "tile", None),
        check_vma=False,
    )
```

```python
import jax
import jax.numpy as jnp
from jax import lax
from jax.experimental import pallas as pl
from jax.experimental.pallas import tpu as pltpu
from jax.sharding import PartitionSpec as P

ROUNDS = 6


def from_behind(value, axis, by):
    count = lax.axis_size(axis)
    pairs = [(i, i + by) for i in range(count) if 0 <= i + by < count]
    return lax.ppermute(value, axis, pairs)


def exchange_kernel(
    masked, by_row, chosen, south, north, south_courant, north_courant,
    total, received, send_sems, recv_sems,
):
    mesh = pl.DeviceIdType.MESH
    tiles = lax.axis_size("tile")
    bits = lax.axis_size("group").bit_length() - 1
    tile = lax.axis_index("tile")
    me = lax.axis_index("group")
    core = me % 2
    half = masked.shape[0] // 2
    planes = south_courant.shape[0]
    halo = south_courant.shape[1]
    rows_from = chosen.shape[1] - halo
    up = by_row.at[pl.ds(by_row.shape[0] - halo, halo)]
    down = by_row.at[pl.ds(0, halo)]

    def partner(bit):
        return me + (1 << bit) * (1 - 2 * ((me // (1 << bit)) % 2))

    barrier = pltpu.get_barrier_semaphore()
    for bit in range(bits):
        pl.semaphore_signal(barrier, 1, device_id=(tile, partner(bit)), device_id_type=mesh)

    @pl.when(tile > 0)
    def _():
        pl.semaphore_signal(barrier, 1, device_id=(tile - 1, me), device_id_type=mesh)

    @pl.when(tile < tiles - 1)
    def _():
        pl.semaphore_signal(barrier, 1, device_id=(tile + 1, me), device_id_type=mesh)

    has_south = (tile + tiles - 1) // tiles
    has_north = (2 * tiles - 3 - tile) // (tiles - 1)
    pl.semaphore_wait(barrier, bits + has_south + has_north)

    def along_tile(source, target, slot, by):
        return pltpu.make_async_remote_copy(
            src_ref=source, dst_ref=target, send_sem=send_sems.at[slot],
            recv_sem=recv_sems.at[slot], device_id=(tile + by, me), device_id_type=mesh,
        )

    @pl.when(tile == 0)
    def _():
        south[...] = jnp.zeros_like(south)
        south_courant[...] = jnp.zeros_like(south_courant)

    @pl.when(tile == tiles - 1)
    def _():
        north[...] = jnp.zeros_like(north)
        north_courant[...] = jnp.zeros_like(north_courant)

    def along_group(source, bit, slot):
        copy = pltpu.make_async_remote_copy(
            src_ref=source, dst_ref=received.at[slot], send_sem=send_sems.at[2 + slot],
            recv_sem=recv_sems.at[2 + slot], device_id=(tile, partner(bit)),
            device_id_type=mesh,
        )
        copy.start()
        copy.wait()

    along_group(masked.at[pl.ds((1 - core) * half, half)], 0, 0)
    total[...] = masked[pl.ds(core * half, half)] + received[0]
    for bit in range(1, bits):
        along_group(total, bit, bit)
        total[...] = total[...] + received[bit]
        if bit == 1:
            @pl.when(tile < tiles - 1)
            def _():
                along_tile(up, south, 0, 1).start()

            @pl.when(tile > 0)
            def _():
                along_tile(down, north, 1, -1).start()
    along_group(total, 0, bits)
    chosen[pl.ds(core * half, half)] = total[...]
    chosen[pl.ds((1 - core) * half, half)] = received[bits]

    @pl.when(tile < tiles - 1)
    def _():
        along_tile(chosen.at[pl.ds(0, planes), pl.ds(rows_from, halo)], south_courant, 2 + bits + 1, 1).start()

    @pl.when(tile > 0)
    def _():
        along_tile(chosen.at[pl.ds(0, planes), pl.ds(0, halo)], north_courant, 2 + bits + 2, -1).start()

    @pl.when(tile < tiles - 1)
    def _():
        along_tile(up, south, 0, 1).wait_send()
        along_tile(chosen.at[pl.ds(0, planes), pl.ds(rows_from, halo)], south_courant, 2 + bits + 1, 1).wait_send()
        along_tile(up, north, 1, 1).wait_recv()
        along_tile(chosen.at[pl.ds(0, planes), pl.ds(0, halo)], north_courant, 2 + bits + 2, 1).wait_recv()

    @pl.when(tile > 0)
    def _():
        along_tile(down, north, 1, -1).wait_send()
        along_tile(chosen.at[pl.ds(0, planes), pl.ds(0, halo)], north_courant, 2 + bits + 2, -1).wait_send()
        along_tile(down, south, 0, -1).wait_recv()
        along_tile(chosen.at[pl.ds(0, planes), pl.ds(rows_from, halo)], south_courant, 2 + bits + 1, -1).wait_recv()


def exchange(value, by_row, root, halo, planes):
    groups = lax.axis_size("group")
    assert groups & (groups - 1) == 0 and groups >= 2
    bits = groups.bit_length() - 1
    half = -(-value.shape[0] // 2)
    padded = jnp.concatenate(
        [value, jnp.zeros((2 * half - value.shape[0],) + value.shape[1:], value.dtype)]
    )
    masked = jnp.where(lax.axis_index("group") == root, padded, jnp.zeros_like(padded))
    height = by_row.shape[0]
    vmem = pl.BlockSpec(memory_space=pltpu.VMEM)
    rows = jax.ShapeDtypeStruct((halo,) + by_row.shape[1:], by_row.dtype)
    winds = jax.ShapeDtypeStruct((planes, halo) + value.shape[2:], value.dtype)
    return pl.pallas_call(
        exchange_kernel,
        out_shape=(jax.ShapeDtypeStruct(padded.shape, padded.dtype), rows, rows, winds, winds),
        in_specs=[vmem] * 2,
        out_specs=(vmem,) * 5,
        scratch_shapes=[
            pltpu.VMEM((half,) + value.shape[1:], value.dtype),
            pltpu.VMEM((bits + 1, half) + value.shape[1:], value.dtype),
            pltpu.SemaphoreType.DMA((bits + 5,)),
            pltpu.SemaphoreType.DMA((bits + 5,)),
        ],
        compiler_params=pltpu.CompilerParams(collective_id=0, has_side_effects=True),
    )(masked, by_row)


def transport_kernel(
    substeps, own, south, north, chosen, south_courant, north_courant, emissions, out,
    held, pivots, ratios, lowers, planes, fractions,
):
    levels, height, tracer_count, width = held.shape
    halo = south.shape[0]
    rows = height + 2 * halo
    lane_shape = (tracer_count, width)

    def spread(row_ref, row):
        return jnp.broadcast_to(row_ref[pl.ds(row, 1), :], lane_shape)

    tiles = substeps.shape[0]
    tile_position = lax.axis_index("tile")
    courant = chosen
    coefficient = chosen.at[pl.ds(2 * levels, levels - 1)]

    def _prepare():
        bands = (
            jnp.maximum(tile_position - 1, 0),
            tile_position,
            jnp.minimum(tile_position + 1, tiles - 1),
        )
        for band, position in enumerate(bands):
            count = substeps[position]
            spread_count = jnp.full(lane_shape, count.astype(jnp.float32))
            for substep in range(ROUNDS):
                fractions[3 * substep + band] = jnp.where(
                    substep < count, 1.0 / spread_count, jnp.float32(0.0)
                )
        zero_plane = jnp.zeros((height, width), jnp.float32)
        previous_ratio = zero_plane
        for lev in range(levels):
            lower_coef = coefficient[lev - 1] if lev > 0 else zero_plane
            upper_coef = coefficient[lev] if lev < levels - 1 else zero_plane
            pivot = 1.0 / (1.0 + lower_coef + upper_coef - lower_coef * previous_ratio)
            previous_ratio = upper_coef * pivot
            planes[0] = pivot
            planes[1] = previous_ratio
            planes[2] = lower_coef
            for row in range(height):
                pivots[lev, row] = spread(planes.at[0], row)
                ratios[lev, row] = spread(planes.at[1], row)
                lowers[lev, row] = spread(planes.at[2], row)

    _prepare()

    def advect(level, carry):
        def wind_row(component, row):
            index = component * levels + level
            if row < halo:
                return spread(south_courant.at[index], row)
            if row < halo + height:
                return spread(courant.at[index], row - halo)
            return spread(north_courant.at[index], row - halo - height)

        first_row = jnp.where(tile_position > 0, jnp.float32(1.0), jnp.float32(0.0))
        zonal_up, zonal_down, merid_up, merid_down = [], [], [], []
        for row in range(rows):
            zonal = wind_row(0, row)
            meridional = wind_row(1, row)
            if row == halo:
                meridional = meridional * first_row
            zonal_up.append(jnp.maximum(zonal, 0.0))
            zonal_down.append(jnp.minimum(zonal, 0.0))
            merid_up.append(jnp.maximum(meridional, 0.0))
            merid_down.append(jnp.minimum(meridional, 0.0))

        mixing = [south[row, level] for row in range(halo)]
        mixing += [own[row, level] for row in range(height)]
        mixing += [north[row, level] for row in range(halo)]
        for substep in range(ROUNDS):
            low, high = substep + 1, rows - 2 - substep
            south_flux = {}
            for row in range(low, high + 2):
                south_flux[row] = merid_up[row] * mixing[row - 1] + merid_down[row] * mixing[row]
            advanced = list(mixing)
            for row in range(low, high + 1):
                band = 0 if row < halo else (1 if row < halo + height else 2)
                fraction = fractions[3 * substep + band]
                from_west = pltpu.roll(mixing[row], 1, 1)
                west_flux = zonal_up[row] * from_west + zonal_down[row] * mixing[row]
                east_flux = pltpu.roll(west_flux, width - 1, 1)
                advanced[row] = mixing[row] - fraction * (
                    (east_flux - west_flux) + (south_flux[row + 1] - south_flux[row])
                )
            mixing = advanced
        for row in range(height):
            held[level, row] = mixing[halo + row]
        return carry

    lax.fori_loop(0, levels, advect, 0)

    def _finish():
        for row in range(height):
            held[0, row] = held[0, row] + emissions[row]
            previous_value = jnp.zeros(lane_shape, jnp.float32)
            for lev in range(levels):
                previous_value = (
                    held[lev, row] + lowers[lev, row] * previous_value
                ) * pivots[lev, row]
                held[lev, row] = previous_value
            current = held[levels - 1, row]
            out[row, levels - 1] = current
            for lev in range(levels - 2, -1, -1):
                current = held[lev, row] + ratios[lev, row] * current
                out[row, lev] = current

    _finish()


def transport(substeps, own, south, north, chosen, south_courant, north_courant,
              emissions):
    height, levels, tracer_count, width = own.shape
    vmem = pl.BlockSpec(memory_space=pltpu.VMEM)
    table = pltpu.VMEM((levels, height, tracer_count, width), jnp.float32)
    return pl.pallas_call(
        transport_kernel,
        out_shape=jax.ShapeDtypeStruct(own.shape, jnp.float32),
        in_specs=[pl.BlockSpec(memory_space=pltpu.SMEM)] + [vmem] * 7,
        out_specs=vmem,
        scratch_shapes=[
            table,
            table,
            table,
            table,
            pltpu.VMEM((3, height, width), jnp.float32),
            pltpu.VMEM((3 * ROUNDS, tracer_count, width), jnp.float32),
        ],
        cost_estimate=pl.CostEstimate(
            flops=levels * tracer_count * width * 78 * 14,
            bytes_accessed=4 * (2 * own.size + 2 * south.size + chosen.size),
            transcendentals=0,
        ),
    )(substeps, own, south, north, chosen, south_courant, north_courant, emissions)


def shards(tracers, emissions, winds, diffusivity, substeps, loader):
    tiles = lax.axis_size("tile")
    tile_position = lax.axis_index("tile")
    tile_numbers = jnp.arange(substeps.shape[0])
    loader_slot = jnp.sum(jnp.where(tile_numbers == tile_position, loader, 0))
    levels = tracers.shape[1]
    height = tracers.shape[2]
    width = tracers.shape[3]
    halo = ROUNDS

    local = jnp.concatenate(
        [winds[0].reshape(2 * levels, height, width), diffusivity[0]], axis=0
    )
    by_row = jnp.transpose(tracers, (2, 1, 0, 3))
    chosen, south_rows, north_rows, south_courant, north_courant = exchange(
        local, by_row, loader_slot, halo, 2 * levels
    )
    mixed = transport(
        substeps, by_row, south_rows, north_rows, chosen, south_courant,
        north_courant, jnp.transpose(emissions, (1, 0, 2)),
    )
    return jnp.transpose(mixed, (2, 1, 0, 3))


def solution(mesh):
    return jax.shard_map(
        shards,
        mesh=mesh,
        in_specs=(
            P("group", None, "tile", None),
            P("group", "tile", None),
            P("group", None, None, "tile", None),
            P("group", None, "tile", None),
            P(),
            P(),
        ),
        out_specs=P("group", None, "tile", None),
        check_vma=False,
    )
```

```python
import jax
import jax.numpy as jnp
from jax import lax
from jax.experimental import pallas as pl
from jax.experimental.pallas import tpu as pltpu
from jax.sharding import PartitionSpec as P

ROUNDS = 6


def from_behind(value, axis, by):
    count = lax.axis_size(axis)
    pairs = [(i, i + by) for i in range(count) if 0 <= i + by < count]
    return lax.ppermute(value, axis, pairs)


def exchange_kernel(
    masked, up, down, chosen, south, north, south_courant, north_courant,
    total, received, send_sems, recv_sems,
):
    mesh = pl.DeviceIdType.MESH
    tiles = lax.axis_size("tile")
    bits = lax.axis_size("group").bit_length() - 1
    tile = lax.axis_index("tile")
    me = lax.axis_index("group")
    core = me % 2
    half = masked.shape[0] // 2
    planes = south_courant.shape[0]
    halo = south_courant.shape[1]
    rows_from = chosen.shape[1] - halo

    def partner(bit):
        return me + (1 << bit) * (1 - 2 * ((me // (1 << bit)) % 2))

    barrier = pltpu.get_barrier_semaphore()
    for bit in range(bits):
        pl.semaphore_signal(barrier, 1, device_id=(tile, partner(bit)), device_id_type=mesh)

    @pl.when(tile > 0)
    def _():
        pl.semaphore_signal(barrier, 1, device_id=(tile - 1, me), device_id_type=mesh)

    @pl.when(tile < tiles - 1)
    def _():
        pl.semaphore_signal(barrier, 1, device_id=(tile + 1, me), device_id_type=mesh)

    has_south = (tile + tiles - 1) // tiles
    has_north = (2 * tiles - 3 - tile) // (tiles - 1)
    pl.semaphore_wait(barrier, bits + has_south + has_north)

    def along_tile(source, target, slot, by):
        return pltpu.make_async_remote_copy(
            src_ref=source, dst_ref=target, send_sem=send_sems.at[slot],
            recv_sem=recv_sems.at[slot], device_id=(tile + by, me), device_id_type=mesh,
        )

    @pl.when(tile == 0)
    def _():
        south[...] = jnp.zeros_like(south)
        south_courant[...] = jnp.zeros_like(south_courant)

    @pl.when(tile == tiles - 1)
    def _():
        north[...] = jnp.zeros_like(north)
        north_courant[...] = jnp.zeros_like(north_courant)

    def along_group(source, bit, slot):
        copy = pltpu.make_async_remote_copy(
            src_ref=source, dst_ref=received.at[slot], send_sem=send_sems.at[2 + slot],
            recv_sem=recv_sems.at[2 + slot], device_id=(tile, partner(bit)),
            device_id_type=mesh,
        )
        copy.start()
        copy.wait()

    along_group(masked.at[pl.ds((1 - core) * half, half)], 0, 0)
    total[...] = masked[pl.ds(core * half, half)] + received[0]
    for bit in range(1, bits):
        along_group(total, bit, bit)
        total[...] = total[...] + received[bit]
        if bit == 1:
            @pl.when(tile < tiles - 1)
            def _():
                along_tile(up, south, 0, 1).start()

            @pl.when(tile > 0)
            def _():
                along_tile(down, north, 1, -1).start()
    along_group(total, 0, bits)
    chosen[pl.ds(core * half, half)] = total[...]
    chosen[pl.ds((1 - core) * half, half)] = received[bits]

    @pl.when(tile < tiles - 1)
    def _():
        along_tile(chosen.at[pl.ds(0, planes), pl.ds(rows_from, halo)], south_courant, 2 + bits + 1, 1).start()

    @pl.when(tile > 0)
    def _():
        along_tile(chosen.at[pl.ds(0, planes), pl.ds(0, halo)], north_courant, 2 + bits + 2, -1).start()

    @pl.when(tile < tiles - 1)
    def _():
        along_tile(up, south, 0, 1).wait_send()
        along_tile(chosen.at[pl.ds(0, planes), pl.ds(rows_from, halo)], south_courant, 2 + bits + 1, 1).wait_send()
        along_tile(up, north, 1, 1).wait_recv()
        along_tile(chosen.at[pl.ds(0, planes), pl.ds(0, halo)], north_courant, 2 + bits + 2, 1).wait_recv()

    @pl.when(tile > 0)
    def _():
        along_tile(down, north, 1, -1).wait_send()
        along_tile(chosen.at[pl.ds(0, planes), pl.ds(0, halo)], north_courant, 2 + bits + 2, -1).wait_send()
        along_tile(down, south, 0, -1).wait_recv()
        along_tile(chosen.at[pl.ds(0, planes), pl.ds(rows_from, halo)], south_courant, 2 + bits + 1, -1).wait_recv()


def exchange(value, by_row, root, halo, planes):
    groups = lax.axis_size("group")
    assert groups & (groups - 1) == 0 and groups >= 2
    bits = groups.bit_length() - 1
    half = -(-value.shape[0] // 2)
    padded = jnp.concatenate(
        [value, jnp.zeros((2 * half - value.shape[0],) + value.shape[1:], value.dtype)]
    )
    masked = jnp.where(lax.axis_index("group") == root, padded, jnp.zeros_like(padded))
    height = by_row.shape[0]
    vmem = pl.BlockSpec(memory_space=pltpu.VMEM)
    rows = jax.ShapeDtypeStruct((halo,) + by_row.shape[1:], by_row.dtype)
    winds = jax.ShapeDtypeStruct((planes, halo) + value.shape[2:], value.dtype)
    return pl.pallas_call(
        exchange_kernel,
        out_shape=(jax.ShapeDtypeStruct(padded.shape, padded.dtype), rows, rows, winds, winds),
        in_specs=[vmem] * 3,
        out_specs=(vmem,) * 5,
        scratch_shapes=[
            pltpu.VMEM((half,) + value.shape[1:], value.dtype),
            pltpu.VMEM((bits + 1, half) + value.shape[1:], value.dtype),
            pltpu.SemaphoreType.DMA((bits + 5,)),
            pltpu.SemaphoreType.DMA((bits + 5,)),
        ],
        compiler_params=pltpu.CompilerParams(collective_id=0, has_side_effects=True),
    )(masked, by_row[height - halo :], by_row[:halo])


def transport_kernel(
    substeps, own, south, north, chosen, south_courant, north_courant, emissions, out,
    held, pivots, ratios, lowers, planes, fractions,
):
    levels, height, tracer_count, width = held.shape
    halo = south.shape[0]
    rows = height + 2 * halo
    lane_shape = (tracer_count, width)

    def spread(row_ref, row):
        return jnp.broadcast_to(row_ref[pl.ds(row, 1), :], lane_shape)

    tiles = substeps.shape[0]
    tile_position = lax.axis_index("tile")
    courant = chosen
    coefficient = chosen.at[pl.ds(2 * levels, levels - 1)]

    def _prepare():
        bands = (
            jnp.maximum(tile_position - 1, 0),
            tile_position,
            jnp.minimum(tile_position + 1, tiles - 1),
        )
        for band, position in enumerate(bands):
            count = substeps[position]
            spread_count = jnp.full(lane_shape, count.astype(jnp.float32))
            for substep in range(ROUNDS):
                fractions[3 * substep + band] = jnp.where(
                    substep < count, 1.0 / spread_count, jnp.float32(0.0)
                )
        zero_plane = jnp.zeros((height, width), jnp.float32)
        previous_ratio = zero_plane
        for lev in range(levels):
            lower_coef = coefficient[lev - 1] if lev > 0 else zero_plane
            upper_coef = coefficient[lev] if lev < levels - 1 else zero_plane
            pivot = 1.0 / (1.0 + lower_coef + upper_coef - lower_coef * previous_ratio)
            previous_ratio = upper_coef * pivot
            planes[0] = pivot
            planes[1] = previous_ratio
            planes[2] = lower_coef
            for row in range(height):
                pivots[lev, row] = spread(planes.at[0], row)
                ratios[lev, row] = spread(planes.at[1], row)
                lowers[lev, row] = spread(planes.at[2], row)

    _prepare()

    def advect(level, carry):
        def wind_row(component, row):
            index = component * levels + level
            if row < halo:
                return spread(south_courant.at[index], row)
            if row < halo + height:
                return spread(courant.at[index], row - halo)
            return spread(north_courant.at[index], row - halo - height)

        first_row = jnp.where(tile_position > 0, jnp.float32(1.0), jnp.float32(0.0))
        zonal_up, zonal_down, merid_up, merid_down = [], [], [], []
        for row in range(rows):
            zonal = wind_row(0, row)
            meridional = wind_row(1, row)
            if row == halo:
                meridional = meridional * first_row
            zonal_up.append(jnp.maximum(zonal, 0.0))
            zonal_down.append(jnp.minimum(zonal, 0.0))
            merid_up.append(jnp.maximum(meridional, 0.0))
            merid_down.append(jnp.minimum(meridional, 0.0))

        mixing = [south[row, level] for row in range(halo)]
        mixing += [own[row, level] for row in range(height)]
        mixing += [north[row, level] for row in range(halo)]
        for substep in range(ROUNDS):
            low, high = substep + 1, rows - 2 - substep
            south_flux = {}
            for row in range(low, high + 2):
                south_flux[row] = merid_up[row] * mixing[row - 1] + merid_down[row] * mixing[row]
            advanced = list(mixing)
            for row in range(low, high + 1):
                band = 0 if row < halo else (1 if row < halo + height else 2)
                fraction = fractions[3 * substep + band]
                from_west = pltpu.roll(mixing[row], 1, 1)
                west_flux = zonal_up[row] * from_west + zonal_down[row] * mixing[row]
                east_flux = pltpu.roll(west_flux, width - 1, 1)
                advanced[row] = mixing[row] - fraction * (
                    (east_flux - west_flux) + (south_flux[row + 1] - south_flux[row])
                )
            mixing = advanced
        for row in range(height):
            held[level, row] = mixing[halo + row]
        return carry

    lax.fori_loop(0, levels, advect, 0)

    def _finish():
        for row in range(height):
            held[0, row] = held[0, row] + emissions[row]
            previous_value = jnp.zeros(lane_shape, jnp.float32)
            for lev in range(levels):
                previous_value = (
                    held[lev, row] + lowers[lev, row] * previous_value
                ) * pivots[lev, row]
                held[lev, row] = previous_value

    _finish()

    current = [held[levels - 1, row] for row in range(height)]
    out[:, levels - 1] = jnp.swapaxes(jnp.stack(current), 0, 1)
    for lev in range(levels - 2, -1, -1):
        current = [held[lev, row] + ratios[lev, row] * current[row] for row in range(height)]
        out[:, lev] = jnp.swapaxes(jnp.stack(current), 0, 1)


def transport(substeps, own, south, north, chosen, south_courant, north_courant,
              emissions):
    height, levels, tracer_count, width = own.shape
    vmem = pl.BlockSpec(memory_space=pltpu.VMEM)
    table = pltpu.VMEM((levels, height, tracer_count, width), jnp.float32)
    return pl.pallas_call(
        transport_kernel,
        out_shape=jax.ShapeDtypeStruct((tracer_count, levels, height, width), jnp.float32),
        in_specs=[pl.BlockSpec(memory_space=pltpu.SMEM)] + [vmem] * 7,
        out_specs=vmem,
        scratch_shapes=[
            table,
            table,
            table,
            table,
            pltpu.VMEM((3, height, width), jnp.float32),
            pltpu.VMEM((3 * ROUNDS, tracer_count, width), jnp.float32),
        ],
        cost_estimate=pl.CostEstimate(
            flops=levels * tracer_count * width * 78 * 14,
            bytes_accessed=4 * (2 * own.size + 2 * south.size + chosen.size),
            transcendentals=0,
        ),
    )(substeps, own, south, north, chosen, south_courant, north_courant, emissions)


def shards(tracers, emissions, winds, diffusivity, substeps, loader):
    tiles = lax.axis_size("tile")
    tile_position = lax.axis_index("tile")
    tile_numbers = jnp.arange(substeps.shape[0])
    loader_slot = jnp.sum(jnp.where(tile_numbers == tile_position, loader, 0))
    levels = tracers.shape[1]
    height = tracers.shape[2]
    width = tracers.shape[3]
    halo = ROUNDS

    local = jnp.concatenate(
        [winds[0].reshape(2 * levels, height, width), diffusivity[0]], axis=0
    )
    by_row = jnp.transpose(tracers, (2, 1, 0, 3))
    chosen, south_rows, north_rows, south_courant, north_courant = exchange(
        local, by_row, loader_slot, halo, 2 * levels
    )
    mixed = transport(
        substeps, by_row, south_rows, north_rows, chosen, south_courant,
        north_courant, jnp.transpose(emissions, (1, 0, 2)),
    )
    return mixed


def solution(mesh):
    return jax.shard_map(
        shards,
        mesh=mesh,
        in_specs=(
            P("group", None, "tile", None),
            P("group", "tile", None),
            P("group", None, None, "tile", None),
            P("group", None, "tile", None),
            P(),
            P(),
        ),
        out_specs=P("group", None, "tile", None),
        check_vma=False,
    )
```

```python
import jax
import jax.numpy as jnp
from jax import lax
from jax.experimental import pallas as pl
from jax.experimental.pallas import tpu as pltpu
from jax.sharding import PartitionSpec as P

ROUNDS = 6


def from_behind(value, axis, by):
    count = lax.axis_size(axis)
    pairs = [(i, i + by) for i in range(count) if 0 <= i + by < count]
    return lax.ppermute(value, axis, pairs)


def exchange_kernel(
    masked, tracers, chosen, by_row, south, north, south_courant, north_courant,
    total, received, send_sems, recv_sems,
):
    mesh = pl.DeviceIdType.MESH
    tiles = lax.axis_size("tile")
    bits = lax.axis_size("group").bit_length() - 1
    tile = lax.axis_index("tile")
    me = lax.axis_index("group")
    core = me % 2
    half = masked.shape[0] // 2
    planes = south_courant.shape[0]
    halo = south_courant.shape[1]
    rows_from = chosen.shape[1] - halo
    up = by_row.at[pl.ds(by_row.shape[0] - halo, halo)]
    down = by_row.at[pl.ds(0, halo)]

    def partner(bit):
        return me + (1 << bit) * (1 - 2 * ((me // (1 << bit)) % 2))

    barrier = pltpu.get_barrier_semaphore()
    for bit in range(bits):
        pl.semaphore_signal(barrier, 1, device_id=(tile, partner(bit)), device_id_type=mesh)

    @pl.when(tile > 0)
    def _():
        pl.semaphore_signal(barrier, 1, device_id=(tile - 1, me), device_id_type=mesh)

    @pl.when(tile < tiles - 1)
    def _():
        pl.semaphore_signal(barrier, 1, device_id=(tile + 1, me), device_id_type=mesh)

    has_south = (tile + tiles - 1) // tiles
    has_north = (2 * tiles - 3 - tile) // (tiles - 1)
    pl.semaphore_wait(barrier, bits + has_south + has_north)

    def along_tile(source, target, slot, by):
        return pltpu.make_async_remote_copy(
            src_ref=source, dst_ref=target, send_sem=send_sems.at[slot],
            recv_sem=recv_sems.at[slot], device_id=(tile + by, me), device_id_type=mesh,
        )

    @pl.when(tile == 0)
    def _():
        south[...] = jnp.zeros_like(south)
        south_courant[...] = jnp.zeros_like(south_courant)

    @pl.when(tile == tiles - 1)
    def _():
        north[...] = jnp.zeros_like(north)
        north_courant[...] = jnp.zeros_like(north_courant)

    def along_group(source, bit, slot):
        copy = pltpu.make_async_remote_copy(
            src_ref=source, dst_ref=received.at[slot], send_sem=send_sems.at[2 + slot],
            recv_sem=recv_sems.at[2 + slot], device_id=(tile, partner(bit)),
            device_id_type=mesh,
        )
        copy.start()
        return copy

    first = along_group(masked.at[pl.ds((1 - core) * half, half)], 0, 0)
    for level in range(tracers.shape[1]):
        by_row[:, level] = jnp.swapaxes(tracers[:, level], 0, 1)
    first.wait()
    total[...] = masked[pl.ds(core * half, half)] + received[0]
    for bit in range(1, bits):
        along_group(total, bit, bit).wait()
        total[...] = total[...] + received[bit]
        if bit == 1:
            @pl.when(tile < tiles - 1)
            def _():
                along_tile(up, south, 0, 1).start()

            @pl.when(tile > 0)
            def _():
                along_tile(down, north, 1, -1).start()
    along_group(total, 0, bits).wait()
    chosen[pl.ds(core * half, half)] = total[...]
    chosen[pl.ds((1 - core) * half, half)] = received[bits]

    @pl.when(tile < tiles - 1)
    def _():
        along_tile(chosen.at[pl.ds(0, planes), pl.ds(rows_from, halo)], south_courant, 2 + bits + 1, 1).start()

    @pl.when(tile > 0)
    def _():
        along_tile(chosen.at[pl.ds(0, planes), pl.ds(0, halo)], north_courant, 2 + bits + 2, -1).start()

    @pl.when(tile < tiles - 1)
    def _():
        along_tile(up, south, 0, 1).wait_send()
        along_tile(chosen.at[pl.ds(0, planes), pl.ds(rows_from, halo)], south_courant, 2 + bits + 1, 1).wait_send()
        along_tile(up, north, 1, 1).wait_recv()
        along_tile(chosen.at[pl.ds(0, planes), pl.ds(0, halo)], north_courant, 2 + bits + 2, 1).wait_recv()

    @pl.when(tile > 0)
    def _():
        along_tile(down, north, 1, -1).wait_send()
        along_tile(chosen.at[pl.ds(0, planes), pl.ds(0, halo)], north_courant, 2 + bits + 2, -1).wait_send()
        along_tile(down, south, 0, -1).wait_recv()
        along_tile(chosen.at[pl.ds(0, planes), pl.ds(rows_from, halo)], south_courant, 2 + bits + 1, -1).wait_recv()


def exchange(value, tracers, root, halo, planes):
    groups = lax.axis_size("group")
    assert groups & (groups - 1) == 0 and groups >= 2
    bits = groups.bit_length() - 1
    half = -(-value.shape[0] // 2)
    padded = jnp.concatenate(
        [value, jnp.zeros((2 * half - value.shape[0],) + value.shape[1:], value.dtype)]
    )
    masked = jnp.where(lax.axis_index("group") == root, padded, jnp.zeros_like(padded))
    tracer_count, levels, height, width = tracers.shape
    vmem = pl.BlockSpec(memory_space=pltpu.VMEM)
    by_row = jax.ShapeDtypeStruct((height, levels, tracer_count, width), tracers.dtype)
    rows = jax.ShapeDtypeStruct((halo, levels, tracer_count, width), tracers.dtype)
    winds = jax.ShapeDtypeStruct((planes, halo) + value.shape[2:], value.dtype)
    return pl.pallas_call(
        exchange_kernel,
        out_shape=(jax.ShapeDtypeStruct(padded.shape, padded.dtype), by_row, rows, rows, winds, winds),
        in_specs=[vmem] * 2,
        out_specs=(vmem,) * 6,
        scratch_shapes=[
            pltpu.VMEM((half,) + value.shape[1:], value.dtype),
            pltpu.VMEM((bits + 1, half) + value.shape[1:], value.dtype),
            pltpu.SemaphoreType.DMA((bits + 5,)),
            pltpu.SemaphoreType.DMA((bits + 5,)),
        ],
        compiler_params=pltpu.CompilerParams(collective_id=0, has_side_effects=True),
    )(masked, tracers)


def transport_kernel(
    substeps, own, south, north, chosen, south_courant, north_courant, emissions, out,
    held, pivots, ratios, lowers, planes, fractions,
):
    levels, height, tracer_count, width = held.shape
    halo = south.shape[0]
    rows = height + 2 * halo
    lane_shape = (tracer_count, width)

    def spread(row_ref, row):
        return jnp.broadcast_to(row_ref[pl.ds(row, 1), :], lane_shape)

    tiles = substeps.shape[0]
    tile_position = lax.axis_index("tile")
    courant = chosen
    coefficient = chosen.at[pl.ds(2 * levels, levels - 1)]

    def _prepare():
        bands = (
            jnp.maximum(tile_position - 1, 0),
            tile_position,
            jnp.minimum(tile_position + 1, tiles - 1),
        )
        for band, position in enumerate(bands):
            count = substeps[position]
            spread_count = jnp.full(lane_shape, count.astype(jnp.float32))
            for substep in range(ROUNDS):
                fractions[3 * substep + band] = jnp.where(
                    substep < count, 1.0 / spread_count, jnp.float32(0.0)
                )
        zero_plane = jnp.zeros((height, width), jnp.float32)
        previous_ratio = zero_plane
        for lev in range(levels):
            lower_coef = coefficient[lev - 1] if lev > 0 else zero_plane
            upper_coef = coefficient[lev] if lev < levels - 1 else zero_plane
            pivot = 1.0 / (1.0 + lower_coef + upper_coef - lower_coef * previous_ratio)
            previous_ratio = upper_coef * pivot
            planes[0] = pivot
            planes[1] = previous_ratio
            planes[2] = lower_coef
            for row in range(height):
                pivots[lev, row] = spread(planes.at[0], row)
                ratios[lev, row] = spread(planes.at[1], row)
                lowers[lev, row] = spread(planes.at[2], row)

    _prepare()

    def advect(level, carry):
        def wind_row(component, row):
            index = component * levels + level
            if row < halo:
                return spread(south_courant.at[index], row)
            if row < halo + height:
                return spread(courant.at[index], row - halo)
            return spread(north_courant.at[index], row - halo - height)

        first_row = jnp.where(tile_position > 0, jnp.float32(1.0), jnp.float32(0.0))
        zonal_up, zonal_down, merid_up, merid_down = [], [], [], []
        for row in range(rows):
            zonal = wind_row(0, row)
            meridional = wind_row(1, row)
            if row == halo:
                meridional = meridional * first_row
            zonal_up.append(jnp.maximum(zonal, 0.0))
            zonal_down.append(jnp.minimum(zonal, 0.0))
            merid_up.append(jnp.maximum(meridional, 0.0))
            merid_down.append(jnp.minimum(meridional, 0.0))

        mixing = [south[row, level] for row in range(halo)]
        mixing += [own[row, level] for row in range(height)]
        mixing += [north[row, level] for row in range(halo)]
        for substep in range(ROUNDS):
            low, high = substep + 1, rows - 2 - substep
            south_flux = {}
            for row in range(low, high + 2):
                south_flux[row] = merid_up[row] * mixing[row - 1] + merid_down[row] * mixing[row]
            advanced = list(mixing)
            for row in range(low, high + 1):
                band = 0 if row < halo else (1 if row < halo + height else 2)
                fraction = fractions[3 * substep + band]
                from_west = pltpu.roll(mixing[row], 1, 1)
                west_flux = zonal_up[row] * from_west + zonal_down[row] * mixing[row]
                east_flux = pltpu.roll(west_flux, width - 1, 1)
                advanced[row] = mixing[row] - fraction * (
                    (east_flux - west_flux) + (south_flux[row + 1] - south_flux[row])
                )
            mixing = advanced
        for row in range(height):
            held[level, row] = mixing[halo + row]
        return carry

    lax.fori_loop(0, levels, advect, 0)

    def _finish():
        sources = jnp.swapaxes(emissions[...], 0, 1)
        for row in range(height):
            held[0, row] = held[0, row] + sources[row]
            previous_value = jnp.zeros(lane_shape, jnp.float32)
            for lev in range(levels):
                previous_value = (
                    held[lev, row] + lowers[lev, row] * previous_value
                ) * pivots[lev, row]
                held[lev, row] = previous_value

    _finish()

    current = [held[levels - 1, row] for row in range(height)]
    out[:, levels - 1] = jnp.swapaxes(jnp.stack(current), 0, 1)
    for lev in range(levels - 2, -1, -1):
        current = [held[lev, row] + ratios[lev, row] * current[row] for row in range(height)]
        out[:, lev] = jnp.swapaxes(jnp.stack(current), 0, 1)


def transport(substeps, own, south, north, chosen, south_courant, north_courant,
              emissions):
    height, levels, tracer_count, width = own.shape
    vmem = pl.BlockSpec(memory_space=pltpu.VMEM)
    table = pltpu.VMEM((levels, height, tracer_count, width), jnp.float32)
    return pl.pallas_call(
        transport_kernel,
        out_shape=jax.ShapeDtypeStruct((tracer_count, levels, height, width), jnp.float32),
        in_specs=[pl.BlockSpec(memory_space=pltpu.SMEM)] + [vmem] * 7,
        out_specs=vmem,
        scratch_shapes=[
            table,
            table,
            table,
            table,
            pltpu.VMEM((3, height, width), jnp.float32),
            pltpu.VMEM((3 * ROUNDS, tracer_count, width), jnp.float32),
        ],
        cost_estimate=pl.CostEstimate(
            flops=levels * tracer_count * width * 78 * 14,
            bytes_accessed=4 * (2 * own.size + 2 * south.size + chosen.size),
            transcendentals=0,
        ),
    )(substeps, own, south, north, chosen, south_courant, north_courant, emissions)


def shards(tracers, emissions, winds, diffusivity, substeps, loader):
    tiles = lax.axis_size("tile")
    tile_position = lax.axis_index("tile")
    tile_numbers = jnp.arange(substeps.shape[0])
    loader_slot = jnp.sum(jnp.where(tile_numbers == tile_position, loader, 0))
    levels = tracers.shape[1]
    height = tracers.shape[2]
    width = tracers.shape[3]
    halo = ROUNDS

    local = jnp.concatenate(
        [winds[0].reshape(2 * levels, height, width), diffusivity[0]], axis=0
    )
    chosen, by_row, south_rows, north_rows, south_courant, north_courant = exchange(
        local, tracers, loader_slot, halo, 2 * levels
    )
    mixed = transport(
        substeps, by_row, south_rows, north_rows, chosen, south_courant,
        north_courant, emissions,
    )
    return mixed


def solution(mesh):
    return jax.shard_map(
        shards,
        mesh=mesh,
        in_specs=(
            P("group", None, "tile", None),
            P("group", "tile", None),
            P("group", None, None, "tile", None),
            P("group", None, "tile", None),
            P(),
            P(),
        ),
        out_specs=P("group", None, "tile", None),
        check_vma=False,
    )
```

```python
import jax
import jax.numpy as jnp
from jax import lax
from jax.experimental import pallas as pl
from jax.experimental.pallas import tpu as pltpu
from jax.sharding import PartitionSpec as P

ROUNDS = 6


def from_behind(value, axis, by):
    count = lax.axis_size(axis)
    pairs = [(i, i + by) for i in range(count) if 0 <= i + by < count]
    return lax.ppermute(value, axis, pairs)


def exchange_kernel(
    scale, courant_in, coefficient_in, tracers, chosen, by_row, south, north,
    south_courant, north_courant, masked, total, received, send_sems, recv_sems,
):
    mesh = pl.DeviceIdType.MESH
    tiles = lax.axis_size("tile")
    bits = lax.axis_size("group").bit_length() - 1
    tile = lax.axis_index("tile")
    me = lax.axis_index("group")
    core = me % 2
    half = masked.shape[0] // 2
    weight = scale[0]
    count = courant_in.shape[0]
    masked[pl.ds(0, count)] = courant_in[...] * weight
    masked[pl.ds(count, coefficient_in.shape[0])] = coefficient_in[...] * weight
    masked[pl.ds(count + coefficient_in.shape[0], masked.shape[0] - count - coefficient_in.shape[0])] = jnp.zeros(
        (masked.shape[0] - count - coefficient_in.shape[0],) + masked.shape[1:], jnp.float32
    )
    planes = south_courant.shape[0]
    halo = south_courant.shape[1]
    rows_from = chosen.shape[1] - halo
    up = by_row.at[pl.ds(by_row.shape[0] - halo, halo)]
    down = by_row.at[pl.ds(0, halo)]

    def partner(bit):
        return me + (1 << bit) * (1 - 2 * ((me // (1 << bit)) % 2))

    barrier = pltpu.get_barrier_semaphore()
    for bit in range(bits):
        pl.semaphore_signal(barrier, 1, device_id=(tile, partner(bit)), device_id_type=mesh)

    @pl.when(tile > 0)
    def _():
        pl.semaphore_signal(barrier, 1, device_id=(tile - 1, me), device_id_type=mesh)

    @pl.when(tile < tiles - 1)
    def _():
        pl.semaphore_signal(barrier, 1, device_id=(tile + 1, me), device_id_type=mesh)

    has_south = (tile + tiles - 1) // tiles
    has_north = (2 * tiles - 3 - tile) // (tiles - 1)
    pl.semaphore_wait(barrier, bits + has_south + has_north)

    def along_tile(source, target, slot, by):
        return pltpu.make_async_remote_copy(
            src_ref=source, dst_ref=target, send_sem=send_sems.at[slot],
            recv_sem=recv_sems.at[slot], device_id=(tile + by, me), device_id_type=mesh,
        )

    @pl.when(tile == 0)
    def _():
        south[...] = jnp.zeros_like(south)
        south_courant[...] = jnp.zeros_like(south_courant)

    @pl.when(tile == tiles - 1)
    def _():
        north[...] = jnp.zeros_like(north)
        north_courant[...] = jnp.zeros_like(north_courant)

    def along_group(source, bit, slot):
        copy = pltpu.make_async_remote_copy(
            src_ref=source, dst_ref=received.at[slot], send_sem=send_sems.at[2 + slot],
            recv_sem=recv_sems.at[2 + slot], device_id=(tile, partner(bit)),
            device_id_type=mesh,
        )
        copy.start()
        return copy

    first = along_group(masked.at[pl.ds((1 - core) * half, half)], 0, 0)
    for level in range(tracers.shape[1]):
        by_row[:, level] = jnp.swapaxes(tracers[:, level], 0, 1)
    first.wait()
    total[...] = masked[pl.ds(core * half, half)] + received[0]
    for bit in range(1, bits):
        along_group(total, bit, bit).wait()
        total[...] = total[...] + received[bit]
        if bit == 1:
            @pl.when(tile < tiles - 1)
            def _():
                along_tile(up, south, 0, 1).start()

            @pl.when(tile > 0)
            def _():
                along_tile(down, north, 1, -1).start()
    along_group(total, 0, bits).wait()
    chosen[pl.ds(core * half, half)] = total[...]
    chosen[pl.ds((1 - core) * half, half)] = received[bits]

    @pl.when(tile < tiles - 1)
    def _():
        along_tile(chosen.at[pl.ds(0, planes), pl.ds(rows_from, halo)], south_courant, 2 + bits + 1, 1).start()

    @pl.when(tile > 0)
    def _():
        along_tile(chosen.at[pl.ds(0, planes), pl.ds(0, halo)], north_courant, 2 + bits + 2, -1).start()

    @pl.when(tile < tiles - 1)
    def _():
        along_tile(up, south, 0, 1).wait_send()
        along_tile(chosen.at[pl.ds(0, planes), pl.ds(rows_from, halo)], south_courant, 2 + bits + 1, 1).wait_send()
        along_tile(up, north, 1, 1).wait_recv()
        along_tile(chosen.at[pl.ds(0, planes), pl.ds(0, halo)], north_courant, 2 + bits + 2, 1).wait_recv()

    @pl.when(tile > 0)
    def _():
        along_tile(down, north, 1, -1).wait_send()
        along_tile(chosen.at[pl.ds(0, planes), pl.ds(0, halo)], north_courant, 2 + bits + 2, -1).wait_send()
        along_tile(down, south, 0, -1).wait_recv()
        along_tile(chosen.at[pl.ds(0, planes), pl.ds(rows_from, halo)], south_courant, 2 + bits + 1, -1).wait_recv()


def exchange(courant, coefficient, tracers, root, halo):
    groups = lax.axis_size("group")
    assert groups & (groups - 1) == 0 and groups >= 2
    bits = groups.bit_length() - 1
    planes = courant.shape[0]
    half = -(-(planes + coefficient.shape[0]) // 2)
    scale = jnp.where(lax.axis_index("group") == root, jnp.float32(1.0), jnp.float32(0.0))
    tracer_count, levels, height, width = tracers.shape
    vmem = pl.BlockSpec(memory_space=pltpu.VMEM)
    by_row = jax.ShapeDtypeStruct((height, levels, tracer_count, width), tracers.dtype)
    rows = jax.ShapeDtypeStruct((halo, levels, tracer_count, width), tracers.dtype)
    winds = jax.ShapeDtypeStruct((planes, halo, width), courant.dtype)
    return pl.pallas_call(
        exchange_kernel,
        out_shape=(
            jax.ShapeDtypeStruct((2 * half,) + courant.shape[1:], courant.dtype),
            by_row, rows, rows, winds, winds,
        ),
        in_specs=[pl.BlockSpec(memory_space=pltpu.SMEM)] + [vmem] * 3,
        out_specs=(vmem,) * 6,
        scratch_shapes=[
            pltpu.VMEM((2 * half,) + courant.shape[1:], courant.dtype),
            pltpu.VMEM((half,) + courant.shape[1:], courant.dtype),
            pltpu.VMEM((bits + 1, half) + courant.shape[1:], courant.dtype),
            pltpu.SemaphoreType.DMA((bits + 5,)),
            pltpu.SemaphoreType.DMA((bits + 5,)),
        ],
        compiler_params=pltpu.CompilerParams(collective_id=0, has_side_effects=True),
    )(scale[None], courant, coefficient, tracers)


def transport_kernel(
    substeps, own, south, north, chosen, south_courant, north_courant, emissions, out,
    held, pivots, ratios, lowers, planes, fractions,
):
    levels, height, tracer_count, width = held.shape
    halo = south.shape[0]
    rows = height + 2 * halo
    lane_shape = (tracer_count, width)

    def spread(row_ref, row):
        return jnp.broadcast_to(row_ref[pl.ds(row, 1), :], lane_shape)

    tiles = substeps.shape[0]
    tile_position = lax.axis_index("tile")
    courant = chosen
    coefficient = chosen.at[pl.ds(2 * levels, levels - 1)]

    def _prepare():
        bands = (
            jnp.maximum(tile_position - 1, 0),
            tile_position,
            jnp.minimum(tile_position + 1, tiles - 1),
        )
        for band, position in enumerate(bands):
            count = substeps[position]
            spread_count = jnp.full(lane_shape, count.astype(jnp.float32))
            for substep in range(ROUNDS):
                fractions[3 * substep + band] = jnp.where(
                    substep < count, 1.0 / spread_count, jnp.float32(0.0)
                )
        zero_plane = jnp.zeros((height, width), jnp.float32)
        previous_ratio = zero_plane
        for lev in range(levels):
            lower_coef = coefficient[lev - 1] if lev > 0 else zero_plane
            upper_coef = coefficient[lev] if lev < levels - 1 else zero_plane
            pivot = 1.0 / (1.0 + lower_coef + upper_coef - lower_coef * previous_ratio)
            previous_ratio = upper_coef * pivot
            planes[0] = pivot
            planes[1] = previous_ratio
            planes[2] = lower_coef
            for row in range(height):
                pivots[lev, row] = spread(planes.at[0], row)
                ratios[lev, row] = spread(planes.at[1], row)
                lowers[lev, row] = spread(planes.at[2], row)

    _prepare()

    def advect(level, carry):
        def wind_row(component, row):
            index = component * levels + level
            if row < halo:
                return spread(south_courant.at[index], row)
            if row < halo + height:
                return spread(courant.at[index], row - halo)
            return spread(north_courant.at[index], row - halo - height)

        first_row = jnp.where(tile_position > 0, jnp.float32(1.0), jnp.float32(0.0))
        zonal_up, zonal_down, merid_up, merid_down = [], [], [], []
        for row in range(rows):
            zonal = wind_row(0, row)
            meridional = wind_row(1, row)
            if row == halo:
                meridional = meridional * first_row
            zonal_up.append(jnp.maximum(zonal, 0.0))
            zonal_down.append(jnp.minimum(zonal, 0.0))
            merid_up.append(jnp.maximum(meridional, 0.0))
            merid_down.append(jnp.minimum(meridional, 0.0))

        mixing = [south[row, level] for row in range(halo)]
        mixing += [own[row, level] for row in range(height)]
        mixing += [north[row, level] for row in range(halo)]
        for substep in range(ROUNDS):
            low, high = substep + 1, rows - 2 - substep
            south_flux = {}
            for row in range(low, high + 2):
                south_flux[row] = merid_up[row] * mixing[row - 1] + merid_down[row] * mixing[row]
            advanced = list(mixing)
            for row in range(low, high + 1):
                band = 0 if row < halo else (1 if row < halo + height else 2)
                fraction = fractions[3 * substep + band]
                from_west = pltpu.roll(mixing[row], 1, 1)
                west_flux = zonal_up[row] * from_west + zonal_down[row] * mixing[row]
                east_flux = pltpu.roll(west_flux, width - 1, 1)
                advanced[row] = mixing[row] - fraction * (
                    (east_flux - west_flux) + (south_flux[row + 1] - south_flux[row])
                )
            mixing = advanced
        for row in range(height):
            held[level, row] = mixing[halo + row]
        return carry

    lax.fori_loop(0, levels, advect, 0)

    def _finish():
        sources = jnp.swapaxes(emissions[...], 0, 1)
        for row in range(height):
            held[0, row] = held[0, row] + sources[row]
            previous_value = jnp.zeros(lane_shape, jnp.float32)
            for lev in range(levels):
                previous_value = (
                    held[lev, row] + lowers[lev, row] * previous_value
                ) * pivots[lev, row]
                held[lev, row] = previous_value

    _finish()

    current = [held[levels - 1, row] for row in range(height)]
    out[:, levels - 1] = jnp.swapaxes(jnp.stack(current), 0, 1)
    for lev in range(levels - 2, -1, -1):
        current = [held[lev, row] + ratios[lev, row] * current[row] for row in range(height)]
        out[:, lev] = jnp.swapaxes(jnp.stack(current), 0, 1)


def transport(substeps, own, south, north, chosen, south_courant, north_courant,
              emissions):
    height, levels, tracer_count, width = own.shape
    vmem = pl.BlockSpec(memory_space=pltpu.VMEM)
    table = pltpu.VMEM((levels, height, tracer_count, width), jnp.float32)
    return pl.pallas_call(
        transport_kernel,
        out_shape=jax.ShapeDtypeStruct((tracer_count, levels, height, width), jnp.float32),
        in_specs=[pl.BlockSpec(memory_space=pltpu.SMEM)] + [vmem] * 7,
        out_specs=vmem,
        scratch_shapes=[
            table,
            table,
            table,
            table,
            pltpu.VMEM((3, height, width), jnp.float32),
            pltpu.VMEM((3 * ROUNDS, tracer_count, width), jnp.float32),
        ],
        cost_estimate=pl.CostEstimate(
            flops=levels * tracer_count * width * 78 * 14,
            bytes_accessed=4 * (2 * own.size + 2 * south.size + chosen.size),
            transcendentals=0,
        ),
    )(substeps, own, south, north, chosen, south_courant, north_courant, emissions)


def shards(tracers, emissions, winds, diffusivity, substeps, loader):
    tiles = lax.axis_size("tile")
    tile_position = lax.axis_index("tile")
    tile_numbers = jnp.arange(substeps.shape[0])
    loader_slot = jnp.sum(jnp.where(tile_numbers == tile_position, loader, 0))
    levels = tracers.shape[1]
    height = tracers.shape[2]
    width = tracers.shape[3]
    halo = ROUNDS

    chosen, by_row, south_rows, north_rows, south_courant, north_courant = exchange(
        winds[0].reshape(2 * levels, height, width), diffusivity[0], tracers, loader_slot, halo
    )
    mixed = transport(
        substeps, by_row, south_rows, north_rows, chosen, south_courant,
        north_courant, emissions,
    )
    return mixed


def solution(mesh):
    return jax.shard_map(
        shards,
        mesh=mesh,
        in_specs=(
            P("group", None, "tile", None),
            P("group", "tile", None),
            P("group", None, None, "tile", None),
            P("group", None, "tile", None),
            P(),
            P(),
        ),
        out_specs=P("group", None, "tile", None),
        check_vma=False,
    )
```

```python
import jax
import jax.numpy as jnp
from jax import lax
from jax.experimental import pallas as pl
from jax.experimental.pallas import tpu as pltpu
from jax.sharding import PartitionSpec as P

ROUNDS = 6


def from_behind(value, axis, by):
    count = lax.axis_size(axis)
    pairs = [(i, i + by) for i in range(count) if 0 <= i + by < count]
    return lax.ppermute(value, axis, pairs)


def exchange_kernel(
    scale, courant_in, coefficient_in, tracers, chosen, by_row, south, north,
    south_courant, north_courant, masked, total, received, send_sems, recv_sems,
):
    mesh = pl.DeviceIdType.MESH
    tiles = lax.axis_size("tile")
    bits = lax.axis_size("group").bit_length() - 1
    tile = lax.axis_index("tile")
    me = lax.axis_index("group")
    core = me % 2
    half = masked.shape[0] // 2
    weight = scale[0]
    count = courant_in.shape[0]
    masked[pl.ds(0, count)] = courant_in[...] * weight
    masked[pl.ds(count, coefficient_in.shape[0])] = coefficient_in[...] * weight
    masked[pl.ds(count + coefficient_in.shape[0], masked.shape[0] - count - coefficient_in.shape[0])] = jnp.zeros(
        (masked.shape[0] - count - coefficient_in.shape[0],) + masked.shape[1:], jnp.float32
    )
    planes = south_courant.shape[0]
    halo = south_courant.shape[1]
    rows_from = chosen.shape[1] - halo
    up = by_row.at[pl.ds(by_row.shape[0] - halo, halo)]
    down = by_row.at[pl.ds(0, halo)]

    def partner(bit):
        return me + (1 << bit) * (1 - 2 * ((me // (1 << bit)) % 2))

    barrier = pltpu.get_barrier_semaphore()
    for bit in range(bits):
        pl.semaphore_signal(barrier, 1, device_id=(tile, partner(bit)), device_id_type=mesh)

    @pl.when(tile > 0)
    def _():
        pl.semaphore_signal(barrier, 1, device_id=(tile - 1, me), device_id_type=mesh)

    @pl.when(tile < tiles - 1)
    def _():
        pl.semaphore_signal(barrier, 1, device_id=(tile + 1, me), device_id_type=mesh)

    has_south = (tile + tiles - 1) // tiles
    has_north = (2 * tiles - 3 - tile) // (tiles - 1)
    pl.semaphore_wait(barrier, bits + has_south + has_north)

    def along_tile(source, target, slot, by):
        return pltpu.make_async_remote_copy(
            src_ref=source, dst_ref=target, send_sem=send_sems.at[slot],
            recv_sem=recv_sems.at[slot], device_id=(tile + by, me), device_id_type=mesh,
        )

    @pl.when(tile == 0)
    def _():
        south[...] = jnp.zeros_like(south)
        south_courant[...] = jnp.zeros_like(south_courant)

    @pl.when(tile == tiles - 1)
    def _():
        north[...] = jnp.zeros_like(north)
        north_courant[...] = jnp.zeros_like(north_courant)

    def along_group(source, bit, slot):
        copy = pltpu.make_async_remote_copy(
            src_ref=source, dst_ref=received.at[slot], send_sem=send_sems.at[2 + slot],
            recv_sem=recv_sems.at[2 + slot], device_id=(tile, partner(bit)),
            device_id_type=mesh,
        )
        copy.start()
        return copy

    levels = tracers.shape[1]
    split = levels // 2

    def swap_levels(low, high):
        for level in range(low, high):
            by_row[:, level] = jnp.swapaxes(tracers[:, level], 0, 1)

    first = along_group(masked.at[pl.ds((1 - core) * half, half)], 0, 0)
    swap_levels(0, split)
    first.wait()
    total[...] = masked[pl.ds(core * half, half)] + received[0]
    for bit in range(1, bits):
        copy = along_group(total, bit, bit)
        if bit == 1:
            swap_levels(split, levels)
        copy.wait()
        total[...] = total[...] + received[bit]
        if bit == 1:
            @pl.when(tile < tiles - 1)
            def _():
                along_tile(up, south, 0, 1).start()

            @pl.when(tile > 0)
            def _():
                along_tile(down, north, 1, -1).start()
    along_group(total, 0, bits).wait()
    chosen[pl.ds(core * half, half)] = total[...]
    chosen[pl.ds((1 - core) * half, half)] = received[bits]

    @pl.when(tile < tiles - 1)
    def _():
        along_tile(chosen.at[pl.ds(0, planes), pl.ds(rows_from, halo)], south_courant, 2 + bits + 1, 1).start()

    @pl.when(tile > 0)
    def _():
        along_tile(chosen.at[pl.ds(0, planes), pl.ds(0, halo)], north_courant, 2 + bits + 2, -1).start()

    @pl.when(tile < tiles - 1)
    def _():
        along_tile(up, south, 0, 1).wait_send()
        along_tile(chosen.at[pl.ds(0, planes), pl.ds(rows_from, halo)], south_courant, 2 + bits + 1, 1).wait_send()
        along_tile(up, north, 1, 1).wait_recv()
        along_tile(chosen.at[pl.ds(0, planes), pl.ds(0, halo)], north_courant, 2 + bits + 2, 1).wait_recv()

    @pl.when(tile > 0)
    def _():
        along_tile(down, north, 1, -1).wait_send()
        along_tile(chosen.at[pl.ds(0, planes), pl.ds(0, halo)], north_courant, 2 + bits + 2, -1).wait_send()
        along_tile(down, south, 0, -1).wait_recv()
        along_tile(chosen.at[pl.ds(0, planes), pl.ds(rows_from, halo)], south_courant, 2 + bits + 1, -1).wait_recv()


def exchange(courant, coefficient, tracers, root, halo):
    groups = lax.axis_size("group")
    assert groups & (groups - 1) == 0 and groups >= 2
    bits = groups.bit_length() - 1
    planes = courant.shape[0]
    half = -(-(planes + coefficient.shape[0]) // 2)
    scale = jnp.where(lax.axis_index("group") == root, jnp.float32(1.0), jnp.float32(0.0))
    tracer_count, levels, height, width = tracers.shape
    vmem = pl.BlockSpec(memory_space=pltpu.VMEM)
    by_row = jax.ShapeDtypeStruct((height, levels, tracer_count, width), tracers.dtype)
    rows = jax.ShapeDtypeStruct((halo, levels, tracer_count, width), tracers.dtype)
    winds = jax.ShapeDtypeStruct((planes, halo, width), courant.dtype)
    return pl.pallas_call(
        exchange_kernel,
        out_shape=(
            jax.ShapeDtypeStruct((2 * half,) + courant.shape[1:], courant.dtype),
            by_row, rows, rows, winds, winds,
        ),
        in_specs=[pl.BlockSpec(memory_space=pltpu.SMEM)] + [vmem] * 3,
        out_specs=(vmem,) * 6,
        scratch_shapes=[
            pltpu.VMEM((2 * half,) + courant.shape[1:], courant.dtype),
            pltpu.VMEM((half,) + courant.shape[1:], courant.dtype),
            pltpu.VMEM((bits + 1, half) + courant.shape[1:], courant.dtype),
            pltpu.SemaphoreType.DMA((bits + 5,)),
            pltpu.SemaphoreType.DMA((bits + 5,)),
        ],
        compiler_params=pltpu.CompilerParams(collective_id=0, has_side_effects=True),
    )(scale[None], courant, coefficient, tracers)


def transport_kernel(
    substeps, own, south, north, chosen, south_courant, north_courant, emissions, out,
    held, pivots, ratios, lowers, planes, fractions,
):
    levels, height, tracer_count, width = held.shape
    halo = south.shape[0]
    rows = height + 2 * halo
    lane_shape = (tracer_count, width)

    def spread(row_ref, row):
        return jnp.broadcast_to(row_ref[pl.ds(row, 1), :], lane_shape)

    tiles = substeps.shape[0]
    tile_position = lax.axis_index("tile")
    courant = chosen
    coefficient = chosen.at[pl.ds(2 * levels, levels - 1)]

    def _prepare():
        bands = (
            jnp.maximum(tile_position - 1, 0),
            tile_position,
            jnp.minimum(tile_position + 1, tiles - 1),
        )
        for band, position in enumerate(bands):
            count = substeps[position]
            spread_count = jnp.full(lane_shape, count.astype(jnp.float32))
            for substep in range(ROUNDS):
                fractions[3 * substep + band] = jnp.where(
                    substep < count, 1.0 / spread_count, jnp.float32(0.0)
                )
        zero_plane = jnp.zeros((height, width), jnp.float32)
        previous_ratio = zero_plane
        for lev in range(levels):
            lower_coef = coefficient[lev - 1] if lev > 0 else zero_plane
            upper_coef = coefficient[lev] if lev < levels - 1 else zero_plane
            pivot = 1.0 / (1.0 + lower_coef + upper_coef - lower_coef * previous_ratio)
            previous_ratio = upper_coef * pivot
            planes[0] = pivot
            planes[1] = previous_ratio
            planes[2] = lower_coef
            for row in range(height):
                pivots[lev, row] = spread(planes.at[0], row)
                ratios[lev, row] = spread(planes.at[1], row)
                lowers[lev, row] = spread(planes.at[2], row)

    _prepare()

    def advect(level, carry):
        def wind_row(component, row):
            index = component * levels + level
            if row < halo:
                return spread(south_courant.at[index], row)
            if row < halo + height:
                return spread(courant.at[index], row - halo)
            return spread(north_courant.at[index], row - halo - height)

        first_row = jnp.where(tile_position > 0, jnp.float32(1.0), jnp.float32(0.0))
        zonal_up, zonal_down, merid_up, merid_down = [], [], [], []
        for row in range(rows):
            zonal = wind_row(0, row)
            meridional = wind_row(1, row)
            if row == halo:
                meridional = meridional * first_row
            zonal_up.append(jnp.maximum(zonal, 0.0))
            zonal_down.append(jnp.minimum(zonal, 0.0))
            merid_up.append(jnp.maximum(meridional, 0.0))
            merid_down.append(jnp.minimum(meridional, 0.0))

        mixing = [south[row, level] for row in range(halo)]
        mixing += [own[row, level] for row in range(height)]
        mixing += [north[row, level] for row in range(halo)]
        for substep in range(ROUNDS):
            low, high = substep + 1, rows - 2 - substep
            south_flux = {}
            for row in range(low, high + 2):
                south_flux[row] = merid_up[row] * mixing[row - 1] + merid_down[row] * mixing[row]
            advanced = list(mixing)
            for row in range(low, high + 1):
                band = 0 if row < halo else (1 if row < halo + height else 2)
                fraction = fractions[3 * substep + band]
                from_west = pltpu.roll(mixing[row], 1, 1)
                west_flux = zonal_up[row] * from_west + zonal_down[row] * mixing[row]
                east_flux = pltpu.roll(west_flux, width - 1, 1)
                advanced[row] = mixing[row] - fraction * (
                    (east_flux - west_flux) + (south_flux[row + 1] - south_flux[row])
                )
            mixing = advanced
        for row in range(height):
            held[level, row] = mixing[halo + row]
        return carry

    lax.fori_loop(0, levels, advect, 0)

    def _finish():
        sources = jnp.swapaxes(emissions[...], 0, 1)
        for row in range(height):
            held[0, row] = held[0, row] + sources[row]
            previous_value = jnp.zeros(lane_shape, jnp.float32)
            for lev in range(levels):
                previous_value = (
                    held[lev, row] + lowers[lev, row] * previous_value
                ) * pivots[lev, row]
                held[lev, row] = previous_value

    _finish()

    current = [held[levels - 1, row] for row in range(height)]
    out[:, levels - 1] = jnp.swapaxes(jnp.stack(current), 0, 1)
    for lev in range(levels - 2, -1, -1):
        current = [held[lev, row] + ratios[lev, row] * current[row] for row in range(height)]
        out[:, lev] = jnp.swapaxes(jnp.stack(current), 0, 1)


def transport(substeps, own, south, north, chosen, south_courant, north_courant,
              emissions):
    height, levels, tracer_count, width = own.shape
    vmem = pl.BlockSpec(memory_space=pltpu.VMEM)
    table = pltpu.VMEM((levels, height, tracer_count, width), jnp.float32)
    return pl.pallas_call(
        transport_kernel,
        out_shape=jax.ShapeDtypeStruct((tracer_count, levels, height, width), jnp.float32),
        in_specs=[pl.BlockSpec(memory_space=pltpu.SMEM)] + [vmem] * 7,
        out_specs=vmem,
        scratch_shapes=[
            table,
            table,
            table,
            table,
            pltpu.VMEM((3, height, width), jnp.float32),
            pltpu.VMEM((3 * ROUNDS, tracer_count, width), jnp.float32),
        ],
        cost_estimate=pl.CostEstimate(
            flops=levels * tracer_count * width * 78 * 14,
            bytes_accessed=4 * (2 * own.size + 2 * south.size + chosen.size),
            transcendentals=0,
        ),
    )(substeps, own, south, north, chosen, south_courant, north_courant, emissions)


def shards(tracers, emissions, winds, diffusivity, substeps, loader):
    tiles = lax.axis_size("tile")
    tile_position = lax.axis_index("tile")
    tile_numbers = jnp.arange(substeps.shape[0])
    loader_slot = jnp.sum(jnp.where(tile_numbers == tile_position, loader, 0))
    levels = tracers.shape[1]
    height = tracers.shape[2]
    width = tracers.shape[3]
    halo = ROUNDS

    chosen, by_row, south_rows, north_rows, south_courant, north_courant = exchange(
        winds[0].reshape(2 * levels, height, width), diffusivity[0], tracers, loader_slot, halo
    )
    mixed = transport(
        substeps, by_row, south_rows, north_rows, chosen, south_courant,
        north_courant, emissions,
    )
    return mixed


def solution(mesh):
    return jax.shard_map(
        shards,
        mesh=mesh,
        in_specs=(
            P("group", None, "tile", None),
            P("group", "tile", None),
            P("group", None, None, "tile", None),
            P("group", None, "tile", None),
            P(),
            P(),
        ),
        out_specs=P("group", None, "tile", None),
        check_vma=False,
    )
```
